128 devices in a mesh: mem: 16 (over z, x_hi, core), lev: 8 (over y, x_lo).
Axes of the slice: x: 4 (x_hi: 2, x_lo: 2; x = x_hi * 2 + x_lo), y: 4, z: 4, core: 2. Of those that a mesh axis runs over, the one named last changes fastest.
Arguments:
- control: float32 [16, 128, 128, 256], P('mem', 'lev'), may hold values from -6 to 6
- diffusivity: float32 [128, 128, 256], P('lev'), may hold values from 0.02 to 0.24
- perturb: float32 [16, 49152, 128], P('mem', 'lev'), may hold values from -6 to 6
- vertical_filter: float32 [128, 128], replicated, may hold values from -0.5 to 0.5
- sub_widths: int32 [8], replicated, may hold values from 1 to 6144, 32768 in all
- obs_raw: int32 [8, 6144], P('lev'), may hold values from 0 to 1048575
- obs_counts: int32 [8], replicated, may hold values from 1 to 6144, 43008 in all
- obs_rinv: float32 [8, 6144, 128], P('lev'), may hold values from 0.3 to 3
Outputs:
- ensemble_term: float32 [16, 128, 128, 256], P('mem', 'lev')
The draws below stay inside these ranges and needn't reach their ends.
Inputs may be any that keep to these rules, and one draw needn't show every extreme that they name: `sub_widths`: the widths sum to 32768; the largest is exactly 6144. `obs_counts`: the counts sum to 43008; the largest is exactly 6144.
All inputs are finite; a program needn't handle non-finite values.
Results may differ from the reference program's by a relative error of at most 0.00011.
Values sent between devices are 32-bit elements; how exact they have to be, the bound alone decides.
A program may use at most 192 MiB of HBM per device.

```python
import math
import jax
import jax.numpy as jnp
import numpy as np
from jax import lax

NX = 128
NY = 256
STEPS = 4
MEM = 16
LEVELS = 128
SUB_CAP = 6144
OBS_CAP = 6144
N_LEV = 8


def plant(entries, key, least, largest):
    longest = entries.shape.index(max(entries.shape))
    spots = []
    for shift in (0, 1):
        where = [jax.random.randint(jax.random.fold_in(key, axis), (), 0, length) for axis, length in enumerate(entries.shape)]
        where[longest] = (where[longest] + shift) % entries.shape[longest]
        spots.append(tuple(where))
    return entries.at[spots[0]].set(least).at[spots[1]].set(largest)


def shard_levels(own_key, shape, split, least, high):
    loudness = 1.0
    for dim, shards_of in split:
        heights = jax.random.uniform(jax.random.fold_in(jax.random.fold_in(own_key, 6), dim), (shards_of,), jnp.float32, least / len(split), high / len(split))
        loudness = loudness * jnp.repeat(jnp.exp(heights), shape[dim] // shards_of).reshape((-1,) + (1,) * (len(shape) - 1 - dim))
    return loudness


def length_profile(amount, total, limit, lean):
    weights = [(1 << 20) // math.isqrt(rank ** lean) + 1 for rank in range(2, amount + 1)]
    spare, holding = total - limit - (amount - 1), [1] * (amount - 1)
    while spare > 0:
        candidates = [i for i in range(amount - 1) if holding[i] < limit]
        pool, remaining = sum([weights[i] for i in candidates]), spare
        for i in candidates:
            more = min(limit - holding[i], max(1, remaining * weights[i] // pool), spare)
            holding[i] = holding[i] + more
            spare = spare - more
    return np.array([limit] + holding)


def uneven(stream_key, amount, total, limit, skew):
    if amount == 2:
        one = jax.random.randint(stream_key, (), max(1, total - limit), min(limit, total - 1) + 1)
        return jnp.stack([one, total - one])
    lengths = jnp.asarray(length_profile(amount, total, limit, skew), jnp.int32)
    pairs = (amount - 1) // 2
    giver, sink = lengths[1:1 + 2 * pairs:2], lengths[2:2 + 2 * pairs:2]
    room = jnp.minimum(giver - 1, limit - sink)
    moved = jax.random.randint(jax.random.fold_in(stream_key, 1), (pairs,), 0, 1 << 20) % (room + 1)
    lengths = lengths.at[1:1 + 2 * pairs:2].set(giver - moved).at[2:2 + 2 * pairs:2].set(sink + moved)
    return lengths[jax.random.permutation(jax.random.fold_in(stream_key, 2), amount)]


def bell_draw(key, dims, spread, most, split=(), held_as=jnp.bfloat16):
    drawn = jax.random.normal(key, dims, jnp.float32) * spread
    if len(split) > 0:
        drawn = shard_levels(key, dims, split, -0.22, 0.18) * drawn
    return jnp.clip(drawn, min=-most, max=most).astype(held_as)


def setup_inputs(seed: int = 0) -> dict:
    seeds = jax.random.split(jax.random.key(seed), 9)
    return {
        "control": bell_draw(seeds[0], (MEM, LEVELS, NX, NY), 1.0, 6.0, ((0, 16), (1, 8)), jnp.float32),
        "diffusivity": jnp.clip(jnp.exp(math.log(0.24) - 2.4849066 * jax.random.uniform(seeds[1], (LEVELS, NX, NY), jnp.float32) ** shard_levels(seeds[1], (LEVELS, NX, NY), ((0, 8),), -0.2, 0.2)), 0.02, 0.24),
        "perturb": bell_draw(seeds[2], (MEM, N_LEV * SUB_CAP, LEVELS), (MEM ** -0.25), 6.0, ((0, 16), (1, 8)), jnp.float32),
        "vertical_filter": bell_draw(seeds[3], (LEVELS, LEVELS), LEVELS ** -0.5, 0.5, (), jnp.float32),
        "sub_widths": uneven(seeds[4], N_LEV, NX * NY, SUB_CAP, 2).astype(jnp.int32),
        "obs_raw": plant(jax.random.randint(seeds[5], (N_LEV, OBS_CAP), 0, 1048576), jax.random.fold_in(seeds[5], 1), 0, 1048575).astype(jnp.int32),
        "obs_counts": uneven(seeds[6], N_LEV, N_LEV * OBS_CAP * 7 // 8, OBS_CAP, 2).astype(jnp.int32),
        "obs_rinv": jnp.clip(jnp.exp(math.log(3.0) - 2.3025851 * jax.random.uniform(seeds[7], (N_LEV, OBS_CAP, LEVELS), jnp.float32) ** shard_levels(seeds[7], (N_LEV, OBS_CAP, LEVELS), ((0, 8),), -0.2, 0.2)), 0.3, 3.0),
    }


def diffuse(values, diffusivity):
    face_x = 0.5 * (diffusivity[..., 1:, :] + diffusivity[..., :-1, :])
    face_y = 0.5 * (diffusivity[..., :, 1:] + diffusivity[..., :, :-1])
    leading = [(0, 0)] * (values.ndim - 2)
    for repeat in range(STEPS):
        flux_x = face_x * (values[..., 1:, :] - values[..., :-1, :])
        flux_y = face_y * (values[..., :, 1:] - values[..., :, :-1])
        padded_x = jnp.pad(flux_x, leading + [(1, 1), (0, 0)])
        padded_y = jnp.pad(flux_y, leading + [(0, 0), (1, 1)])
        values = values + (padded_x[..., 1:, :] - padded_x[..., :-1, :]) + (padded_y[..., :, 1:] - padded_y[..., :, :-1])
    return values


def row_tables(sub_widths, capacity, columns):
    widths = sub_widths.astype(jnp.int32)
    starts = (jnp.cumsum(widths) - widths).astype(jnp.int32)
    rows_all = jnp.arange(widths.shape[0] * capacity, dtype=jnp.int32)
    owner = (rows_all // capacity).astype(jnp.int32)
    offset = (rows_all % capacity).astype(jnp.int32)
    valid = offset < widths[owner]
    target = jnp.where(valid, starts[owner] + offset, columns).astype(jnp.int32)
    source = jnp.minimum(target, columns - 1).astype(jnp.int32)
    return target, source


def reference(control, diffusivity, perturb, vertical_filter, sub_widths, obs_raw, obs_counts, obs_rinv):
    columns = NX * NY
    highest = lax.Precision.HIGHEST
    target, source = row_tables(sub_widths, SUB_CAP, columns)

    def accumulate(total, member):
        member_control, member_perturb = member
        smooth = diffuse(member_control, diffusivity).reshape(LEVELS, columns)
        column_form = jnp.take(smooth, source, axis=1).T
        filtered = jnp.dot(column_form, vertical_filter.T, precision=highest)
        return total + member_perturb * filtered, None

    increment, unused = lax.scan(accumulate, jnp.zeros((N_LEV * SUB_CAP, LEVELS), jnp.float32), (control, perturb))
    widths = sub_widths.astype(jnp.int32)
    slots = (obs_raw.astype(jnp.int32) % widths[:, None]).astype(jnp.int32)
    obs_rows = (jnp.arange(N_LEV, dtype=jnp.int32)[:, None] * SUB_CAP + slots).astype(jnp.int32)
    live = jnp.arange(OBS_CAP, dtype=jnp.int32)[None, :] < obs_counts.astype(jnp.int32)[:, None]
    weighted = jnp.where(live[..., None], obs_rinv * increment[obs_rows], jnp.zeros_like(obs_rinv))
    adjoint_obs = jnp.zeros_like(increment).at[obs_rows.reshape(-1)].add(weighted.reshape(-1, LEVELS))

    def backward(member_perturb):
        back_filtered = jnp.dot(member_perturb * adjoint_obs, vertical_filter, precision=highest)
        grid = jnp.zeros((columns + 1, LEVELS), jnp.float32).at[target].add(back_filtered)[:columns]
        return diffuse(grid.T.reshape(LEVELS, NX, NY), diffusivity)

    return lax.map(backward, perturb)
```

```python
import functools

import jax
import jax.numpy as jnp
from jax import lax
from jax.experimental import pallas as pl
from jax.experimental.pallas import tpu as pltpu
from jax.sharding import PartitionSpec as P

STEPS = 4
LANES = 128


def lane_index(shape):
    return lax.broadcasted_iota(jnp.int32, shape, len(shape) - 1)


def make_faces(diff_ref, face_x, face_y, size_x):
    levels = face_x.shape[1]
    lane = lane_index((levels, LANES))
    load, _ = rows_access(diff_ref, size_x, levels)

    def step(i, here):
        k0, k1 = here
        after = jnp.minimum(i + 1, size_x - 1)
        n0, n1 = load(after, 0), load(after, 1)
        inner = jnp.where(i < size_x - 1, 0.5, 0.0)
        face_x[2 * i] = inner * (k0 + n0)
        face_x[2 * i + 1] = inner * (k1 + n1)
        r0, r1 = pltpu.roll(k0, LANES - 1, 1), pltpu.roll(k1, LANES - 1, 1)
        face_y[2 * i] = 0.5 * (k0 + jnp.where(lane == LANES - 1, r1, r0))
        face_y[2 * i + 1] = jnp.where(lane == LANES - 1, 0.0, 0.5 * (k1 + r1))
        return n0, n1

    lax.fori_loop(0, size_x, step, (load(0, 0), load(0, 1)))


def diffuse_pass(load, store, face_x, face_y, size_x):
    levels = face_x.shape[1]
    lane = lane_index((levels, LANES))
    last, first = lane == LANES - 1, lane == 0
    zero = jnp.zeros((levels, LANES), jnp.float32)

    def step(i, carry):
        v0, v1, above0, above1 = carry
        after = jnp.minimum(i + 1, size_x - 1)
        n0, n1 = load(after, 0), load(after, 1)
        x0 = face_x[2 * i] * (n0 - v0)
        x1 = face_x[2 * i + 1] * (n1 - v1)
        r0, r1 = pltpu.roll(v0, LANES - 1, 1), pltpu.roll(v1, LANES - 1, 1)
        y0 = face_y[2 * i] * (jnp.where(last, r1, r0) - v0)
        y1 = face_y[2 * i + 1] * (r1 - v1)
        b0, b1 = pltpu.roll(y0, 1, 1), pltpu.roll(y1, 1, 1)
        store(i, 0, v0 + (x0 - above0) + (y0 - jnp.where(first, b1, b0)))
        store(i, 1, v1 + (x1 - above1) + (y1 - jnp.where(first, b0, b1)))
        return n0, n1, x0, x1

    lax.fori_loop(0, size_x, step, (load(0, 0), load(0, 1), zero, zero), unroll=2)


def flat_access(ref):
    def load(i, half):
        return ref[2 * i + half]

    def store(i, half, value):
        ref[2 * i + half] = value

    return load, store


def rows_access(ref, size_x, levels):
    def load(i, half):
        return ref[half, pl.ds(i, levels, stride=size_x), :]

    def store(i, half, value):
        ref[half, pl.ds(i, levels, stride=size_x), :] = value

    return load, store


def halves(array, scratch, sems):
    return [
        pltpu.make_async_copy(array.at[:, pl.ds(h * LANES, LANES)], scratch.at[h], sems.at[h])
        for h in range(2)
    ]


def forward_kernel(
    size_x, starts, control_in, diff_in, pieces, face_x, face_y, one, two, control, diff, sems
):
    groups, levels, capacity = pieces.shape
    tiles = 2 * size_x
    diff_copies = halves(diff_in, diff, sems.at[0])
    control_copies = halves(control_in, control, sems.at[1])
    for copy in diff_copies + control_copies:
        copy.start()
    for copy in diff_copies:
        copy.wait()
    make_faces(diff, face_x, face_y, size_x)
    for copy in control_copies:
        copy.wait()
    load_in, _ = rows_access(control, size_x, levels)
    load_one, store_one = flat_access(one)
    load_two, store_two = flat_access(two)
    diffuse_pass(load_in, store_one, face_x, face_y, size_x)
    diffuse_pass(load_one, store_two, face_x, face_y, size_x)
    diffuse_pass(load_two, store_one, face_x, face_y, size_x)
    diffuse_pass(load_one, store_two, face_x, face_y, size_x)
    lane = lane_index((levels, LANES))
    for group in range(groups):
        start = starts[group]
        tile, shift = start // LANES, start % LANES
        keep = lane < LANES - shift
        back = (LANES - shift) % LANES

        def window(q, here):
            after = pltpu.roll(two[jnp.minimum(tile + q + 1, tiles - 1)], back, 1)
            at = pl.multiple_of(q * LANES, LANES)
            pieces[group, :, pl.ds(at, LANES)] = jnp.where(keep, here, after)
            return after

        begin = pltpu.roll(two[jnp.minimum(tile, tiles - 1)], back, 1)
        lax.fori_loop(0, capacity // LANES, window, begin, unroll=4)


def backward_kernel(
    size_x, starts, blocks, diff_in, out_to, face_x, face_y, one, two, out, diff, sems
):
    groups, levels, capacity = blocks.shape
    diff_copies = halves(diff_in, diff, sems.at[0])
    for copy in diff_copies:
        copy.start()
    for copy in diff_copies:
        copy.wait()
    make_faces(diff, face_x, face_y, size_x)
    lane = lane_index((levels, LANES))
    for group in range(groups):
        start = starts[group]
        tile, shift = start // LANES, start % LANES
        keep = lane >= shift

        def place(q, before):
            at = pl.multiple_of(q * LANES, LANES)
            here = pltpu.roll(blocks[group, :, pl.ds(at, LANES)], shift, 1)
            one[tile + q] = jnp.where(keep, here, before)
            return here

        tail = lax.fori_loop(0, capacity // LANES, place, one[tile], unroll=4)
        one[tile + capacity // LANES] = tail
    load_one, store_one = flat_access(one)
    load_two, store_two = flat_access(two)
    _, store_out = rows_access(out, size_x, levels)
    diffuse_pass(load_one, store_two, face_x, face_y, size_x)
    diffuse_pass(load_two, store_one, face_x, face_y, size_x)
    diffuse_pass(load_one, store_two, face_x, face_y, size_x)
    diffuse_pass(load_two, store_out, face_x, face_y, size_x)
    copies = [
        pltpu.make_async_copy(out.at[h], out_to.at[:, pl.ds(h * LANES, LANES)], sems.at[1, h])
        for h in range(2)
    ]
    for copy in copies:
        copy.start()
    for copy in copies:
        copy.wait()


def split_two(values):
    high = values.astype(jnp.bfloat16)
    low = (values - high.astype(jnp.float32)).astype(jnp.bfloat16)
    return high, low


def weights_kernel(base, slots, rinv, out):
    rows = out.shape[0]
    total = rinv.shape[0]
    block = 1024
    acc = jnp.zeros((rows, 2 * LANES), jnp.float32)
    here = base[0] + lax.broadcasted_iota(jnp.int32, (rows, block), 0)
    for k in range(total // block):
        high, low = split_two(rinv[k * block : (k + 1) * block, :])
        chosen = (here == slots[:, k * block : (k + 1) * block]).astype(jnp.bfloat16)
        both = jnp.concatenate([high, low], axis=1)
        acc += jnp.dot(chosen, both, preferred_element_type=jnp.float32)
    out[...] = acc[:, :LANES] + acc[:, LANES:]


SMEM = pl.BlockSpec(memory_space=pltpu.SMEM)
VMEM = pl.BlockSpec(memory_space=pltpu.VMEM)
ANY = pl.BlockSpec(memory_space=pl.ANY)
LIMIT = 60 * 1024 * 1024


def body(control, diffusivity, perturb, vertical_filter, sub_widths, obs_raw, obs_counts, obs_rinv):
    members, levels, size_x, size_y = control.shape
    capacity = perturb.shape[1]
    groups = sub_widths.shape[0]
    tiles = 2 * size_x
    highest = lax.Precision.HIGHEST
    starts = jnp.cumsum(sub_widths) - sub_widths
    diff = diffusivity.reshape(levels * size_x, size_y)
    scratch = [
        pltpu.VMEM((tiles, levels, LANES), jnp.float32),
        pltpu.VMEM((tiles, levels, LANES), jnp.float32),
        pltpu.VMEM((tiles + capacity // LANES + 1, levels, LANES), jnp.float32),
        pltpu.VMEM((tiles, levels, LANES), jnp.float32),
        pltpu.VMEM((2, levels * size_x, LANES), jnp.float32),
        pltpu.VMEM((2, levels * size_x, LANES), jnp.float32),
        pltpu.SemaphoreType.DMA((2, 2)),
    ]
    pieces = pl.pallas_call(
        functools.partial(forward_kernel, size_x),
        out_shape=jax.ShapeDtypeStruct((groups, levels, capacity), jnp.float32),
        in_specs=[SMEM, ANY, ANY],
        out_specs=VMEM,
        scratch_shapes=scratch,
        compiler_params=pltpu.CompilerParams(vmem_limit_bytes=LIMIT),
        name="forward",
    )(starts, control.reshape(levels * size_x, size_y), diff)

    column_form = lax.all_to_all(pieces, "lev", split_axis=0, concat_axis=0, tiled=True)
    column_form = column_form.reshape(groups * levels, capacity)
    filtered = jnp.einsum("ks,lk->sl", column_form, vertical_filter, precision=highest)

    position = lax.axis_index("lev")
    width = sub_widths[position]
    slots = obs_raw % width
    live = jnp.arange(obs_raw.shape[1], dtype=jnp.int32)[None] < obs_counts[position]
    slots = jnp.where(live, slots, -1)
    owned = capacity // lax.axis_size("mem")
    base = (lax.axis_index("mem") * owned).astype(jnp.int32).reshape(1)
    weight = pl.pallas_call(
        weights_kernel,
        out_shape=jax.ShapeDtypeStruct((owned, groups * levels), jnp.float32),
        in_specs=[SMEM, VMEM, VMEM],
        out_specs=VMEM,
        compiler_params=pltpu.CompilerParams(vmem_limit_bytes=LIMIT),
        name="weights",
    )(base, slots, obs_rinv[0])

    part = lax.psum_scatter(perturb[0] * filtered, "mem", scatter_dimension=0, tiled=True)
    adjoint = lax.all_gather(part * weight, "mem", axis=0, tiled=True)
    back = jnp.einsum("sl,lk->ks", perturb[0] * adjoint, vertical_filter, precision=highest)
    blocks = lax.all_to_all(
        back.reshape(groups, levels, capacity), "lev", split_axis=0, concat_axis=0, tiled=True
    )

    out = pl.pallas_call(
        functools.partial(backward_kernel, size_x),
        out_shape=jax.ShapeDtypeStruct((levels * size_x, size_y), jnp.float32),
        in_specs=[SMEM, VMEM, ANY],
        out_specs=ANY,
        scratch_shapes=scratch,
        compiler_params=pltpu.CompilerParams(vmem_limit_bytes=LIMIT),
        name="backward",
    )(starts, blocks, diff)
    return out.reshape(control.shape)


def solution(mesh):
    return jax.shard_map(
        body,
        mesh=mesh,
        in_specs=(
            P("mem", "lev", None, None),
            P("lev", None, None),
            P("mem", "lev", None),
            P(),
            P(),
            P("lev", None),
            P(),
            P("lev", None, None),
        ),
        out_specs=P("mem", "lev", None, None),
        check_vma=False,
    )
```

```python
import functools

import jax
import jax.numpy as jnp
from jax import lax
from jax.experimental import pallas as pl
from jax.experimental.pallas import tpu as pltpu
from jax.sharding import PartitionSpec as P

UNROLL = 16
LANES = 128


CHUNKS = 6
MESH = pl.DeviceIdType.MESH


def lane_index(shape):
    return lax.broadcasted_iota(jnp.int32, shape, len(shape) - 1)


def make_faces(diff_ref, face_x, face_y, size_x):
    levels = face_x.shape[1]
    lane = lane_index((levels, LANES))
    load, _ = rows_access(diff_ref, size_x, levels)

    def step(i, here):
        k0, k1 = here
        after = jnp.minimum(i + 1, size_x - 1)
        n0, n1 = load(after, 0), load(after, 1)
        inner = jnp.where(i < size_x - 1, 0.5, 0.0)
        face_x[2 * i] = inner * (k0 + n0)
        face_x[2 * i + 1] = inner * (k1 + n1)
        r0, r1 = pltpu.roll(k0, LANES - 1, 1), pltpu.roll(k1, LANES - 1, 1)
        face_y[2 * i] = 0.5 * (k0 + jnp.where(lane == LANES - 1, r1, r0))
        face_y[2 * i + 1] = jnp.where(lane == LANES - 1, 0.0, 0.5 * (k1 + r1))
        return n0, n1

    lax.fori_loop(0, size_x, step, (load(0, 0), load(0, 1)), unroll=8)


def diffuse_pass(load, store, face_x, face_y, size_x):
    levels = face_x.shape[1]
    lane = lane_index((levels, LANES))
    last, first = lane == LANES - 1, lane == 0
    zero = jnp.zeros((levels, LANES), jnp.float32)

    def step(i, carry):
        v0, v1, above0, above1 = carry
        after = jnp.minimum(i + 1, size_x - 1)
        n0, n1 = load(after, 0), load(after, 1)
        x0 = face_x[2 * i] * (n0 - v0)
        x1 = face_x[2 * i + 1] * (n1 - v1)
        r0, r1 = pltpu.roll(v0, LANES - 1, 1), pltpu.roll(v1, LANES - 1, 1)
        y0 = face_y[2 * i] * (jnp.where(last, r1, r0) - v0)
        y1 = face_y[2 * i + 1] * (r1 - v1)
        b0, b1 = pltpu.roll(y0, 1, 1), pltpu.roll(y1, 1, 1)
        store(i, 0, v0 + (x0 - above0) + (y0 - jnp.where(first, b1, b0)))
        store(i, 1, v1 + (x1 - above1) + (y1 - jnp.where(first, b0, b1)))
        return n0, n1, x0, x1

    lax.fori_loop(0, size_x, step, (load(0, 0), load(0, 1), zero, zero), unroll=UNROLL)


def flat_access(ref):
    def load(i, half):
        return ref[2 * i + half]

    def store(i, half, value):
        ref[2 * i + half] = value

    return load, store


def rows_access(ref, size_x, levels):
    def load(i, half):
        return ref[half, pl.ds(i, levels, stride=size_x), :]

    def store(i, half, value):
        ref[half, pl.ds(i, levels, stride=size_x), :] = value

    return load, store


def halves(array, scratch, sems):
    return [
        pltpu.make_async_copy(array.at[:, pl.ds(h * LANES, LANES)], scratch.at[h], sems.at[h])
        for h in range(2)
    ]


def forward_kernel(
    size_x,
    widths,
    counts,
    control_in,
    diff_in,
    raw,
    pieces,
    slots,
    face_x,
    face_y,
    one,
    two,
    control,
    diff,
    sems,
):
    groups, levels, capacity = pieces.shape
    tiles = 2 * size_x
    diff_copies = halves(diff_in, diff, sems.at[0])
    control_copies = halves(control_in, control, sems.at[1])
    for copy in diff_copies + control_copies:
        copy.start()
    position = lax.axis_index("lev")
    order = lax.broadcasted_iota(jnp.int32, raw.shape, 0) * LANES + lane_index(raw.shape)
    slots[...] = jnp.where(order < counts[position], lax.rem(raw[...], jnp.full(raw.shape, widths[position])), -1)
    for copy in diff_copies:
        copy.wait()
    make_faces(diff, face_x, face_y, size_x)
    for copy in control_copies:
        copy.wait()
    load_in, _ = rows_access(control, size_x, levels)
    load_one, store_one = flat_access(one)
    load_two, store_two = flat_access(two)
    diffuse_pass(load_in, store_one, face_x, face_y, size_x)
    diffuse_pass(load_one, store_two, face_x, face_y, size_x)
    diffuse_pass(load_two, store_one, face_x, face_y, size_x)
    diffuse_pass(load_one, store_two, face_x, face_y, size_x)
    lane = lane_index((levels, LANES))
    end = jnp.int32(0)
    for group in range(groups):
        start, end = end, end + widths[group]
        tile, shift = start // LANES, start % LANES
        keep = lane < LANES - shift
        back = (LANES - shift) % LANES

        def window(q, here):
            after = pltpu.roll(two[jnp.minimum(tile + q + 1, tiles - 1)], back, 1)
            at = pl.multiple_of(q * LANES, LANES)
            pieces[group, :, pl.ds(at, LANES)] = jnp.where(keep, here, after)
            return after

        begin = pltpu.roll(two[jnp.minimum(tile, tiles - 1)], back, 1)
        lax.fori_loop(0, capacity // LANES, window, begin, unroll=16)


def backward_kernel(
    size_x, widths, blocks, diff_in, out_to, face_x, face_y, one, two, out, diff, sems
):
    groups, levels, capacity = blocks.shape
    diff_copies = halves(diff_in, diff, sems.at[0])
    for copy in diff_copies:
        copy.start()
    for copy in diff_copies:
        copy.wait()
    make_faces(diff, face_x, face_y, size_x)
    lane = lane_index((levels, LANES))
    end = jnp.int32(0)
    for group in range(groups):
        start, end = end, end + widths[group]
        tile, shift = start // LANES, start % LANES
        keep = lane >= shift

        def place(q, before):
            at = pl.multiple_of(q * LANES, LANES)
            here = pltpu.roll(blocks[group, :, pl.ds(at, LANES)], shift, 1)
            one[tile + q] = jnp.where(keep, here, before)
            return here

        tail = lax.fori_loop(0, capacity // LANES, place, one[tile], unroll=16)
        one[tile + capacity // LANES] = tail
    load_one, store_one = flat_access(one)
    load_two, store_two = flat_access(two)
    _, store_out = rows_access(out, size_x, levels)
    diffuse_pass(load_one, store_two, face_x, face_y, size_x)
    diffuse_pass(load_two, store_one, face_x, face_y, size_x)
    diffuse_pass(load_one, store_two, face_x, face_y, size_x)
    diffuse_pass(load_two, store_out, face_x, face_y, size_x)
    copies = [
        pltpu.make_async_copy(out.at[h], out_to.at[:, pl.ds(h * LANES, LANES)], sems.at[1, h])
        for h in range(2)
    ]
    for copy in copies:
        copy.start()
    for copy in copies:
        copy.wait()


def split_two(values):
    high = values.astype(jnp.bfloat16)
    low = (values - high.astype(jnp.float32)).astype(jnp.bfloat16)
    return high, low


def middle_kernel(
    chunks,
    pieces,
    perturb_in,
    rinv_in,
    vertical,
    slots,
    blocks,
    column,
    perturb,
    rinv,
    weight,
    product,
    from_core,
    half,
    from_z,
    eighth,
    from_x,
    adjoint,
    back,
    load_sem,
    in_send,
    in_recv,
    out_send,
    out_recv,
    core_send,
    core_recv,
    z_send,
    z_recv,
    x_send,
    x_recv,
):
    groups, levels, capacity = pieces.shape
    total = groups * levels
    rows = capacity // chunks
    mem, lev = lax.axis_index("mem"), lax.axis_index("lev")
    z, x_hi, core = mem // 4, lax.rem(mem // 2, 2), lax.rem(mem, 2)
    other_core = (mem + 1 - 2 * core, lev)
    other_x = (mem + 2 - 4 * x_hi, lev)
    others_z = [lax.rem(z + d, 4) for d in range(1, 4)]
    across_z = [(there * 4 + x_hi * 2 + core, lev) for there in others_z]
    others_lev = [lax.rem(lev + d, groups) for d in range(1, groups)]
    across_lev = [(mem, there) for there in others_lev]
    sources = [lax.rem(lev + groups - d, groups) for d in range(1, groups)]

    loads = [
        pltpu.make_async_copy(perturb_in, perturb, load_sem.at[0]),
        pltpu.make_async_copy(rinv_in, rinv, load_sem.at[1]),
        pltpu.make_async_copy(pieces.at[lev], column.at[lev], load_sem.at[2]),
    ]
    for copy in loads:
        copy.start()

    barrier = pltpu.get_barrier_semaphore()
    everyone = [other_core, other_x] + across_z + across_lev
    for device in everyone:
        pl.semaphore_signal(barrier, 1, device_id=device, device_id_type=MESH)
    pl.semaphore_wait(barrier, len(everyone))

    pending = []

    def send(source, target, send_sem, recv_sem, device):
        copy = pltpu.make_async_remote_copy(
            source, target, send_sem, recv_sem, device_id=device, device_id_type=MESH
        )
        copy.start()
        pending.append(copy)

    def arrived(target, recv_sem):
        pltpu.make_async_remote_copy(
            target, target, recv_sem, recv_sem, device_id=other_core, device_id_type=MESH
        ).wait_recv()

    def columns(k):
        return pl.ds(k * rows, rows)

    def enter(k):
        for d in range(groups - 1):
            send(
                pieces.at[others_lev[d], :, columns(k)],
                column.at[lev, :, columns(k)],
                in_send.at[k, d],
                in_recv.at[k, d],
                across_lev[d],
            )

    def rows_at(k, *parts):
        first, size = k * rows, rows
        for index, count in parts:
            size = size // count
            first = first + index * size
        return pl.ds(pl.multiple_of(first, 8), size)

    def product_of(high, low, split, contract):
        dims = (((1,), (contract,)), ((), ()))
        v_high, v_low = split
        dot = functools.partial(
            lax.dot_general, dimension_numbers=dims, preferred_element_type=jnp.float32
        )
        return dot(high, v_high) + (dot(high, v_low) + dot(low, v_high))

    enter(0)
    enter(1)

    owned = rows // 16
    block = 512
    first_row = core * (rows // 2) + z * (rows // 8) + x_hi * owned
    here = jnp.concatenate(
        [
            first_row + k * rows + lax.broadcasted_iota(jnp.int32, (owned, LANES), 0)
            for k in range(chunks)
        ],
        axis=0,
    )
    loads[1].wait()
    weight[...] = jnp.zeros_like(weight)

    def gather(b, _):
        high, low = split_two(rinv[pl.ds(pl.multiple_of(b * block, block), block), :])
        mine = slots[pl.ds(b * (block // LANES), block // LANES), :]
        chosen = jnp.concatenate(
            [
                jnp.where(here == mine[q : q + 1, :], 1.0, 0.0).astype(jnp.bfloat16)
                for q in range(block // LANES)
            ],
            axis=1,
        )
        dot = functools.partial(jnp.dot, preferred_element_type=jnp.float32)
        weight[...] += dot(chosen, high) + dot(chosen, low)
        return 0

    lax.fori_loop(0, capacity // block, gather, 0)
    split = split_two(vertical[...])
    loads[0].wait()
    loads[2].wait()
    tile = 256

    def contract_in(k):
        for d in range(groups - 1):
            arrived(column.at[sources[d], :, columns(k)], in_recv.at[k, d])
        if k + 2 < chunks:
            enter(k + 2)

        def one(i, _):
            at = pl.ds(pl.multiple_of(k * rows + i * tile, tile), tile)
            high, low = split_two(column[:, :, at].reshape(total, tile).T)
            product[at, :] = perturb[at, :] * product_of(high, low, split, 1)
            return 0

        lax.fori_loop(0, rows // tile, one, 0)
        there = rows_at(k, (1 - core, 2))
        send(product.at[there], from_core.at[k], core_send.at[0, k], core_recv.at[0, k], other_core)

    def add_core(k):
        arrived(from_core.at[k], core_recv.at[0, k])
        half[k] = product[rows_at(k, (core, 2)), :] + from_core[k]
        for d in range(3):
            quarter = half.at[k, pl.ds(pl.multiple_of(others_z[d] * (rows // 8), 8), rows // 8)]
            send(quarter, from_z.at[k, d], z_send.at[0, k, d], z_recv.at[0, k, d], across_z[d])

    def add_z(k):
        for d in range(3):
            arrived(from_z.at[k, d], z_recv.at[0, k, d])
        own = half[k, pl.ds(pl.multiple_of(z * (rows // 8), 8), rows // 8), :]
        eighth[k] = (own + from_z[k, 0]) + (from_z[k, 1] + from_z[k, 2])
        there = eighth.at[k, pl.ds(pl.multiple_of((1 - x_hi) * owned, 8), owned)]
        send(there, from_x.at[k], x_send.at[0, k], x_recv.at[0, k], other_x)

    def add_x(k):
        arrived(from_x.at[k], x_recv.at[0, k])
        own = eighth[k, pl.ds(pl.multiple_of(x_hi * owned, 8), owned), :]
        at = rows_at(k, (core, 2), (z, 4), (x_hi, 2))
        adjoint[at, :] = (own + from_x[k]) * weight[k * owned : (k + 1) * owned, :]
        send(adjoint.at[at], adjoint.at[at], x_send.at[1, k], x_recv.at[1, k], other_x)

    def give_z(k):
        arrived(adjoint.at[rows_at(k, (core, 2), (z, 4), (1 - x_hi, 2))], x_recv.at[1, k])
        at = rows_at(k, (core, 2), (z, 4))
        for d in range(3):
            send(adjoint.at[at], adjoint.at[at], z_send.at[1, k, d], z_recv.at[1, k, d], across_z[d])

    def give_core(k):
        for d in range(3):
            there = lax.rem(z + 3 - d, 4)
            arrived(adjoint.at[rows_at(k, (core, 2), (there, 4))], z_recv.at[1, k, d])
        at = rows_at(k, (core, 2))
        send(adjoint.at[at], adjoint.at[at], core_send.at[1, k], core_recv.at[1, k], other_core)

    def contract_out(k):
        arrived(adjoint.at[rows_at(k, (1 - core, 2))], core_recv.at[1, k])

        def one(i, _):
            at = pl.ds(pl.multiple_of(k * rows + i * tile, tile), tile)
            high, low = split_two(perturb[at, :] * adjoint[at, :])
            back[:, :, at] = product_of(high, low, split, 0).T.reshape(groups, levels, tile)
            return 0

        lax.fori_loop(0, rows // tile, one, 0)
        for d in range(groups - 1):
            send(
                back.at[others_lev[d], :, columns(k)],
                blocks.at[lev, :, columns(k)],
                out_send.at[k, d],
                out_recv.at[k, d],
                across_lev[d],
            )
        pltpu.make_async_copy(
            back.at[lev, :, columns(k)], blocks.at[lev, :, columns(k)], load_sem.at[3 + k]
        ).start()

    for step in range(chunks + 3):
        for stage, lag in (
            (contract_in, 0),
            (add_z, 1),
            (give_z, 2),
            (add_core, 0),
            (add_x, 1),
            (give_core, 2),
            (contract_out, 3),
        ):
            if 0 <= step - lag < chunks:
                stage(step - lag)

    for k in range(chunks):
        for d in range(groups - 1):
            arrived(blocks.at[sources[d], :, columns(k)], out_recv.at[k, d])
        pltpu.make_async_copy(
            back.at[lev, :, columns(k)], blocks.at[lev, :, columns(k)], load_sem.at[3 + k]
        ).wait()
    for copy in pending:
        copy.wait_send()


SMEM = pl.BlockSpec(memory_space=pltpu.SMEM)
VMEM = pl.BlockSpec(memory_space=pltpu.VMEM)
ANY = pl.BlockSpec(memory_space=pl.ANY)
LIMIT = 60 * 1024 * 1024


def body(control, diffusivity, perturb, vertical_filter, sub_widths, obs_raw, obs_counts, obs_rinv):
    members, levels, size_x, size_y = control.shape
    capacity = perturb.shape[1]
    groups = sub_widths.shape[0]
    tiles = 2 * size_x
    f32 = jnp.float32
    diff = diffusivity.reshape(levels * size_x, size_y)
    scratch = [
        pltpu.VMEM((tiles, levels, LANES), f32),
        pltpu.VMEM((tiles, levels, LANES), f32),
        pltpu.VMEM((tiles + capacity // LANES + 1, levels, LANES), f32),
        pltpu.VMEM((tiles, levels, LANES), f32),
        pltpu.VMEM((2, levels * size_x, LANES), f32),
        pltpu.VMEM((2, levels * size_x, LANES), f32),
        pltpu.SemaphoreType.DMA((2, 2)),
    ]
    lines = capacity // LANES
    pieces, slots = pl.pallas_call(
        functools.partial(forward_kernel, size_x),
        out_shape=(
            jax.ShapeDtypeStruct((groups, levels, capacity), f32),
            jax.ShapeDtypeStruct((lines, LANES), jnp.int32),
        ),
        in_specs=[SMEM, SMEM, ANY, ANY, VMEM],
        out_specs=(VMEM, VMEM),
        scratch_shapes=scratch,
        compiler_params=pltpu.CompilerParams(vmem_limit_bytes=LIMIT),
        name="forward",
    )(
        sub_widths,
        obs_counts,
        control.reshape(levels * size_x, size_y),
        diff,
        obs_raw.reshape(lines, LANES),
    )

    rows = capacity // CHUNKS
    dma = pltpu.SemaphoreType.DMA
    blocks = pl.pallas_call(
        functools.partial(middle_kernel, CHUNKS),
        out_shape=jax.ShapeDtypeStruct((groups, levels, capacity), f32),
        in_specs=[ANY, ANY, ANY, VMEM, VMEM],
        out_specs=VMEM,
        scratch_shapes=[
            pltpu.VMEM((groups, levels, capacity), f32),
            pltpu.VMEM((capacity, LANES), f32),
            pltpu.VMEM((capacity, LANES), f32),
            pltpu.VMEM((capacity // 16, LANES), f32),
            pltpu.VMEM((capacity, LANES), f32),
            pltpu.VMEM((CHUNKS, rows // 2, LANES), f32),
            pltpu.VMEM((CHUNKS, rows // 2, LANES), f32),
            pltpu.VMEM((CHUNKS, 3, rows // 8, LANES), f32),
            pltpu.VMEM((CHUNKS, rows // 8, LANES), f32),
            pltpu.VMEM((CHUNKS, rows // 16, LANES), f32),
            pltpu.VMEM((capacity, LANES), f32),
            pltpu.VMEM((groups, levels, capacity), f32),
            dma((3 + CHUNKS,)),
            dma((CHUNKS, groups - 1)),
            dma((CHUNKS, groups - 1)),
            dma((CHUNKS, groups - 1)),
            dma((CHUNKS, groups - 1)),
            dma((2, CHUNKS)),
            dma((2, CHUNKS)),
            dma((2, CHUNKS, 3)),
            dma((2, CHUNKS, 3)),
            dma((2, CHUNKS)),
            dma((2, CHUNKS)),
        ],
        compiler_params=pltpu.CompilerParams(
            vmem_limit_bytes=LIMIT, collective_id=0, has_side_effects=True
        ),
        name="middle",
    )(pieces, perturb[0], obs_rinv[0], vertical_filter, slots)

    out = pl.pallas_call(
        functools.partial(backward_kernel, size_x),
        out_shape=jax.ShapeDtypeStruct((levels * size_x, size_y), f32),
        in_specs=[SMEM, VMEM, ANY],
        out_specs=ANY,
        scratch_shapes=scratch,
        compiler_params=pltpu.CompilerParams(vmem_limit_bytes=LIMIT),
        name="backward",
    )(sub_widths, blocks, diff)
    return out.reshape(control.shape)


def solution(mesh):
    return jax.shard_map(
        body,
        mesh=mesh,
        in_specs=(
            P("mem", "lev", None, None),
            P("lev", None, None),
            P("mem", "lev", None),
            P(),
            P(),
            P("lev", None),
            P(),
            P("lev", None, None),
        ),
        out_specs=P("mem", "lev", None, None),
        check_vma=False,
    )
```

```python
import functools

import jax
import jax.numpy as jnp
from jax import lax
from jax.experimental import pallas as pl
from jax.experimental.pallas import tpu as pltpu
from jax.sharding import PartitionSpec as P

UNROLL = 32
WINDOW = 48
SUB = 8
LANES = 128


CHUNKS = 8
PACE = 2
SCHED = (("F", 0), ("A", 0), ("B", 1), ("C", 2), ("D", 3), ("E", 4), ("G", 5))
MESH = pl.DeviceIdType.MESH


def lane_index(shape):
    return lax.broadcasted_iota(jnp.int32, shape, len(shape) - 1)


def make_faces(diff, face_x, face_y, size_x, part):
    lane = lane_index((SUB, LANES))
    last = lane == LANES - 1
    at = pl.ds(part * SUB, SUB)

    def step(i, here):
        k0, k1 = here
        n0, n1 = diff[i + 1, 0, at, :], diff[i + 1, 1, at, :]
        face_x[i, 0, at, :] = 0.5 * (k0 + n0)
        face_x[i, 1, at, :] = 0.5 * (k1 + n1)
        r0, r1 = pltpu.roll(k0, LANES - 1, 1), pltpu.roll(k1, LANES - 1, 1)
        face_y[i, 0, at, :] = 0.5 * (k0 + jnp.where(last, r1, r0))
        face_y[i, 1, at, :] = jnp.where(last, 0.0, 0.5 * (k1 + r1))
        return n0, n1

    lax.fori_loop(0, size_x, step, (diff[0, 0, at, :], diff[0, 1, at, :]), unroll=UNROLL)
    face_x[size_x - 1, :, at, :] = jnp.zeros((2, SUB, LANES), jnp.float32)


def clear_edge(ref, first):
    ref[first:] = jnp.zeros((ref.shape[0] - first, *ref.shape[1:]), jnp.float32)


def row_of(ref, i, half):
    return (2 * i + half,) if len(ref.shape) == 3 else (i, half)


def diffuse_pass(source, target, face_x, face_y, size_x, part):
    lane = lane_index((SUB, LANES))
    last, first = lane == LANES - 1, lane == 0
    zero = jnp.zeros((SUB, LANES), jnp.float32)
    at = pl.ds(part * SUB, SUB)

    def step(i, carry):
        v0, v1, above0, above1 = carry
        n0, n1 = (source[*row_of(source, i + 1, half), at, :] for half in range(2))
        x0 = face_x[i, 0, at, :] * (n0 - v0)
        x1 = face_x[i, 1, at, :] * (n1 - v1)
        r0, r1 = pltpu.roll(v0, LANES - 1, 1), pltpu.roll(v1, LANES - 1, 1)
        y0 = face_y[i, 0, at, :] * (jnp.where(last, r1, r0) - v0)
        y1 = face_y[i, 1, at, :] * (r1 - v1)
        b0, b1 = pltpu.roll(y0, 1, 1), pltpu.roll(y1, 1, 1)
        target[*row_of(target, i, 0), at, :] = v0 + (x0 - above0) + (y0 - jnp.where(first, b1, b0))
        target[*row_of(target, i, 1), at, :] = v1 + (x1 - above1) + (y1 - jnp.where(first, b0, b1))
        return n0, n1, x0, x1

    begin = (*(source[*row_of(source, 0, half), at, :] for half in range(2)), zero, zero)
    lax.fori_loop(0, size_x, step, begin, unroll=UNROLL)


def by_level(grid, field, sems, part, out=False):
    size_x = grid.shape[1]
    copies = []
    for level in range(part * SUB, (part + 1) * SUB):
        for half in range(2):
            there = grid.at[level, :, pl.ds(half * LANES, LANES)]
            here = field.at[pl.ds(0, size_x), half, level, :]
            pair = (here, there) if out else (there, here)
            copies.append(pltpu.make_async_copy(*pair, sems.at[level, half]))
    return copies


def forward_kernel(
    widths, counts, control_in, diff_in, raw, pieces, slots, face_x, face_y, control, one, two, diff, sems
):
    groups, levels, capacity = pieces.shape
    size_x = control_in.shape[1]
    tiles = 2 * size_x
    parts = levels // SUB
    diff_copies = [by_level(diff_in, diff, sems.at[0], part) for part in range(parts)]
    control_copies = [by_level(control_in, control, sems.at[1], part) for part in range(parts)]
    for part in range(parts):
        for copy in diff_copies[part] + control_copies[part]:
            copy.start()
    clear_edge(control, size_x)
    clear_edge(one, tiles)
    clear_edge(two, tiles)
    position = lax.axis_index("lev")
    order = lax.broadcasted_iota(jnp.int32, raw.shape, 0) * LANES + lane_index(raw.shape)
    code = lax.rem(raw[...], jnp.full(raw.shape, widths[position]))
    slots[...] = jnp.where(order < counts[position], code, -1)
    lane = lane_index((SUB, LANES))
    for part in range(parts):
        at = pl.ds(part * SUB, SUB)
        for copy in diff_copies[part]:
            copy.wait()
        make_faces(diff, face_x, face_y, size_x, part)
        for copy in control_copies[part]:
            copy.wait()
        for source, target in ((control, two), (two, one), (one, two), (two, one)):
            diffuse_pass(source, target, face_x, face_y, size_x, part)
        end = jnp.int32(0)
        for group in range(groups):
            start, end = end, end + widths[group]
            tile, shift = start // LANES, start % LANES
            keep = lane < LANES - shift
            back = (LANES - shift) % LANES

            def rolled(t):
                return pltpu.roll(one[t, at, :], back, 1)

            def window(q, here):
                after = rolled(tile + q + 1)
                to = pl.multiple_of(q * LANES, LANES)
                pieces[group, at, pl.ds(to, LANES)] = jnp.where(keep, here, after)
                return after

            lax.fori_loop(0, capacity // LANES, window, rolled(tile), unroll=WINDOW)


def backward_kernel(
    widths, blocks, diff_in, out_to, face_x, face_y, one, two, result, diff, sems
):
    groups, levels, capacity = blocks.shape
    size_x = diff_in.shape[1]
    parts = levels // SUB
    diff_copies = [by_level(diff_in, diff, sems.at[0], part) for part in range(parts)]
    for part in range(parts):
        for copy in diff_copies[part]:
            copy.start()
    lane = lane_index((SUB, LANES))
    for part in range(parts):
        at = pl.ds(part * SUB, SUB)
        end = jnp.int32(0)
        for group in range(groups):
            start, end = end, end + widths[group]
            tile, shift = start // LANES, start % LANES
            keep = lane >= shift

            def place(q, before):
                to = pl.multiple_of(q * LANES, LANES)
                here = pltpu.roll(blocks[group, at, pl.ds(to, LANES)], shift, 1)
                one[tile + q, at, :] = jnp.where(keep, here, before)
                return here

            begin = one[tile, at, :]
            tail = lax.fori_loop(0, capacity // LANES, place, begin, unroll=WINDOW)
            one[tile + capacity // LANES, at, :] = tail
    clear_edge(one, 2 * size_x)
    clear_edge(two, 2 * size_x)
    outs = []
    for part in range(parts):
        for copy in diff_copies[part]:
            copy.wait()
        make_faces(diff, face_x, face_y, size_x, part)
        for source, target in ((one, two), (two, one), (one, two), (two, result)):
            diffuse_pass(source, target, face_x, face_y, size_x, part)
        copies = by_level(out_to, result, sems.at[1], part, out=True)
        for copy in copies:
            copy.start()
        outs += copies
    for copy in outs:
        copy.wait()


def split_two(values):
    high = values.astype(jnp.bfloat16)
    low = (values - high.astype(jnp.float32)).astype(jnp.bfloat16)
    return high, low


def middle_kernel(
    chunks,
    pieces,
    perturb_in,
    rinv_in,
    vertical,
    slots,
    blocks,
    column,
    perturb,
    rinv,
    weight,
    product,
    from_core,
    half,
    from_z,
    eighth,
    from_x,
    adjoint,
    back,
    load_sem,
    in_send,
    in_recv,
    out_send,
    out_recv,
    core_send,
    core_recv,
    z_send,
    z_recv,
    x_send,
    x_recv,
):
    groups, levels, capacity = pieces.shape
    total = groups * levels
    rows = capacity // chunks
    mem, lev = lax.axis_index("mem"), lax.axis_index("lev")
    z, x_hi, core = mem // 4, lax.rem(mem // 2, 2), lax.rem(mem, 2)
    other_core = (mem + 1 - 2 * core, lev)
    other_x = (mem + 2 - 4 * x_hi, lev)
    others_z = [lax.rem(z + d, 4) for d in range(1, 4)]
    across_z = [(there * 4 + x_hi * 2 + core, lev) for there in others_z]
    others_lev = [lax.rem(lev + d, groups) for d in range(1, groups)]
    across_lev = [(mem, there) for there in others_lev]
    sources = [lax.rem(lev + groups - d, groups) for d in range(1, groups)]

    loads = [
        pltpu.make_async_copy(perturb_in, perturb, load_sem.at[0]),
        pltpu.make_async_copy(rinv_in, rinv, load_sem.at[1]),
        pltpu.make_async_copy(pieces.at[lev], column.at[lev], load_sem.at[2]),
    ]
    for copy in loads:
        copy.start()

    barrier = pltpu.get_barrier_semaphore()
    everyone = [other_core, other_x] + across_z + across_lev
    for device in everyone:
        pl.semaphore_signal(barrier, 1, device_id=device, device_id_type=MESH)
    pl.semaphore_wait(barrier, len(everyone))

    pending = []

    def send(source, target, send_sem, recv_sem, device):
        copy = pltpu.make_async_remote_copy(
            source, target, send_sem, recv_sem, device_id=device, device_id_type=MESH
        )
        copy.start()
        pending.append(copy)

    def arrived(target, recv_sem):
        pltpu.make_async_remote_copy(
            target, target, recv_sem, recv_sem, device_id=other_core, device_id_type=MESH
        ).wait_recv()

    def columns(k):
        return pl.ds(k * rows, rows)

    def enter(k):
        for d in range(groups - 1):
            send(
                pieces.at[others_lev[d], :, columns(k)],
                column.at[lev, :, columns(k)],
                in_send.at[k, d],
                in_recv.at[k, d],
                across_lev[d],
            )

    def rows_at(k, *parts):
        first, size = k * rows, rows
        for index, count in parts:
            size = size // count
            first = first + index * size
        return pl.ds(pl.multiple_of(first, 8), size)

    def product_of(high, low, split, contract):
        dims = (((1,), (contract,)), ((), ()))
        v_high, v_low = split
        dot = functools.partial(
            lax.dot_general, dimension_numbers=dims, preferred_element_type=jnp.float32
        )
        return dot(high, v_high) + (dot(high, v_low) + dot(low, v_high))

    for k in range(min(PACE, chunks)):
        enter(k)

    owned = rows // 16
    block = 512
    first_row = core * (rows // 2) + z * (rows // 8) + x_hi * owned
    here = jnp.concatenate(
        [
            first_row + k * rows + lax.broadcasted_iota(jnp.int32, (owned, LANES), 0)
            for k in range(chunks)
        ],
        axis=0,
    )
    loads[1].wait()
    weight[...] = jnp.zeros_like(weight)

    def gather(b, _):
        high, low = split_two(rinv[pl.ds(pl.multiple_of(b * block, block), block), :])
        mine = slots[pl.ds(b * (block // LANES), block // LANES), :]
        chosen = jnp.concatenate(
            [
                jnp.where(here == mine[q : q + 1, :], 1.0, 0.0).astype(jnp.bfloat16)
                for q in range(block // LANES)
            ],
            axis=1,
        )
        dot = functools.partial(jnp.dot, preferred_element_type=jnp.float32)
        weight[...] += dot(chosen, high) + dot(chosen, low)
        return 0

    lax.fori_loop(0, capacity // block, gather, 0)
    split = split_two(vertical[...])
    loads[0].wait()
    loads[2].wait()
    tile = 256

    def contract_in(k):
        for d in range(groups - 1):
            arrived(column.at[sources[d], :, columns(k)], in_recv.at[k, d])
        if k + PACE < chunks:
            enter(k + PACE)

        def one(i, _):
            at = pl.ds(pl.multiple_of(k * rows + i * tile, tile), tile)
            high, low = split_two(column[:, :, at].reshape(total, tile).T)
            product[at, :] = perturb[at, :] * product_of(high, low, split, 1)
            return 0

        lax.fori_loop(0, rows // tile, one, 0)
        there = rows_at(k, (1 - core, 2))
        send(product.at[there], from_core.at[k], core_send.at[0, k], core_recv.at[0, k], other_core)

    def add_core(k):
        arrived(from_core.at[k], core_recv.at[0, k])
        half[k] = product[rows_at(k, (core, 2)), :] + from_core[k]
        for d in range(3):
            quarter = half.at[k, pl.ds(pl.multiple_of(others_z[d] * (rows // 8), 8), rows // 8)]
            send(quarter, from_z.at[k, d], z_send.at[0, k, d], z_recv.at[0, k, d], across_z[d])

    def add_z(k):
        for d in range(3):
            arrived(from_z.at[k, d], z_recv.at[0, k, d])
        own = half[k, pl.ds(pl.multiple_of(z * (rows // 8), 8), rows // 8), :]
        eighth[k] = (own + from_z[k, 0]) + (from_z[k, 1] + from_z[k, 2])
        there = eighth.at[k, pl.ds(pl.multiple_of((1 - x_hi) * owned, 8), owned)]
        send(there, from_x.at[k], x_send.at[0, k], x_recv.at[0, k], other_x)

    def add_x(k):
        arrived(from_x.at[k], x_recv.at[0, k])
        own = eighth[k, pl.ds(pl.multiple_of(x_hi * owned, 8), owned), :]
        at = rows_at(k, (core, 2), (z, 4), (x_hi, 2))
        adjoint[at, :] = (own + from_x[k]) * weight[k * owned : (k + 1) * owned, :]
        send(adjoint.at[at], adjoint.at[at], x_send.at[1, k], x_recv.at[1, k], other_x)

    def give_z(k):
        arrived(adjoint.at[rows_at(k, (core, 2), (z, 4), (1 - x_hi, 2))], x_recv.at[1, k])
        at = rows_at(k, (core, 2), (z, 4))
        for d in range(3):
            send(adjoint.at[at], adjoint.at[at], z_send.at[1, k, d], z_recv.at[1, k, d], across_z[d])

    def give_core(k):
        for d in range(3):
            there = lax.rem(z + 3 - d, 4)
            arrived(adjoint.at[rows_at(k, (core, 2), (there, 4))], z_recv.at[1, k, d])
        at = rows_at(k, (core, 2))
        send(adjoint.at[at], adjoint.at[at], core_send.at[1, k], core_recv.at[1, k], other_core)

    def contract_out(k):
        arrived(adjoint.at[rows_at(k, (1 - core, 2))], core_recv.at[1, k])

        def one(i, _):
            at = pl.ds(pl.multiple_of(k * rows + i * tile, tile), tile)
            high, low = split_two(perturb[at, :] * adjoint[at, :])
            back[:, :, at] = product_of(high, low, split, 0).T.reshape(groups, levels, tile)
            return 0

        lax.fori_loop(0, rows // tile, one, 0)
        for d in range(groups - 1):
            send(
                back.at[others_lev[d], :, columns(k)],
                blocks.at[lev, :, columns(k)],
                out_send.at[k, d],
                out_recv.at[k, d],
                across_lev[d],
            )
        pltpu.make_async_copy(
            back.at[lev, :, columns(k)], blocks.at[lev, :, columns(k)], load_sem.at[3 + k]
        ).start()

    stages = dict(F=contract_in, A=add_core, B=add_z, C=add_x, D=give_z, E=give_core, G=contract_out)
    for step in range(chunks + 6):
        for stage, lag in SCHED:
            if 0 <= step - lag < chunks:
                stages[stage](step - lag)

    for k in range(chunks):
        for d in range(groups - 1):
            arrived(blocks.at[sources[d], :, columns(k)], out_recv.at[k, d])
        pltpu.make_async_copy(
            back.at[lev, :, columns(k)], blocks.at[lev, :, columns(k)], load_sem.at[3 + k]
        ).wait()
    for copy in pending:
        copy.wait_send()


SMEM = pl.BlockSpec(memory_space=pltpu.SMEM)
VMEM = pl.BlockSpec(memory_space=pltpu.VMEM)
ANY = pl.BlockSpec(memory_space=pl.ANY)
LIMIT = 60 * 1024 * 1024


def body(control, diffusivity, perturb, vertical_filter, sub_widths, obs_raw, obs_counts, obs_rinv):
    members, levels, size_x, size_y = control.shape
    capacity = perturb.shape[1]
    groups = sub_widths.shape[0]
    f32 = jnp.float32
    field = pltpu.VMEM((size_x + 1, 2, levels, LANES), f32)
    dma = pltpu.SemaphoreType.DMA
    lines = capacity // LANES
    wide = pltpu.VMEM((2 * size_x + lines + 2, levels, LANES), f32)
    pieces, slots = pl.pallas_call(
        forward_kernel,
        out_shape=(
            jax.ShapeDtypeStruct((groups, levels, capacity), f32),
            jax.ShapeDtypeStruct((lines, LANES), jnp.int32),
        ),
        in_specs=[SMEM, SMEM, ANY, ANY, VMEM],
        out_specs=(VMEM, VMEM),
        scratch_shapes=[field, field, field, wide, wide, field, dma((2, levels, 2))],
        compiler_params=pltpu.CompilerParams(vmem_limit_bytes=LIMIT),
        name="forward",
    )(sub_widths, obs_counts, control[0], diffusivity, obs_raw.reshape(lines, LANES))

    rows = capacity // CHUNKS
    blocks = pl.pallas_call(
        functools.partial(middle_kernel, CHUNKS),
        out_shape=jax.ShapeDtypeStruct((groups, levels, capacity), f32),
        in_specs=[ANY, ANY, ANY, VMEM, VMEM],
        out_specs=VMEM,
        scratch_shapes=[
            pltpu.VMEM((groups, levels, capacity), f32),
            pltpu.VMEM((capacity, LANES), f32),
            pltpu.VMEM((capacity, LANES), f32),
            pltpu.VMEM((capacity // 16, LANES), f32),
            pltpu.VMEM((capacity, LANES), f32),
            pltpu.VMEM((CHUNKS, rows // 2, LANES), f32),
            pltpu.VMEM((CHUNKS, rows // 2, LANES), f32),
            pltpu.VMEM((CHUNKS, 3, rows // 8, LANES), f32),
            pltpu.VMEM((CHUNKS, rows // 8, LANES), f32),
            pltpu.VMEM((CHUNKS, rows // 16, LANES), f32),
            pltpu.VMEM((capacity, LANES), f32),
            pltpu.VMEM((groups, levels, capacity), f32),
            dma((3 + CHUNKS,)),
            dma((CHUNKS, groups - 1)),
            dma((CHUNKS, groups - 1)),
            dma((CHUNKS, groups - 1)),
            dma((CHUNKS, groups - 1)),
            dma((2, CHUNKS)),
            dma((2, CHUNKS)),
            dma((2, CHUNKS, 3)),
            dma((2, CHUNKS, 3)),
            dma((2, CHUNKS)),
            dma((2, CHUNKS)),
        ],
        compiler_params=pltpu.CompilerParams(
            vmem_limit_bytes=LIMIT, collective_id=0, has_side_effects=True
        ),
        name="middle",
    )(pieces, perturb[0], obs_rinv[0], vertical_filter, slots)

    out = pl.pallas_call(
        backward_kernel,
        out_shape=jax.ShapeDtypeStruct((levels, size_x, size_y), f32),
        in_specs=[SMEM, VMEM, ANY],
        out_specs=ANY,
        scratch_shapes=[field, field, wide, wide, field, field, dma((2, levels, 2))],
        compiler_params=pltpu.CompilerParams(vmem_limit_bytes=LIMIT),
        name="backward",
    )(sub_widths, blocks, diffusivity)
    return out.reshape(control.shape)


def solution(mesh):
    return jax.shard_map(
        body,
        mesh=mesh,
        in_specs=(
            P("mem", "lev", None, None),
            P("lev", None, None),
            P("mem", "lev", None),
            P(),
            P(),
            P("lev", None),
            P(),
            P("lev", None, None),
        ),
        out_specs=P("mem", "lev", None, None),
        check_vma=False,
    )
```

```python
import functools

import jax
import jax.numpy as jnp
from jax import lax
from jax.experimental import pallas as pl
from jax.experimental.pallas import tpu as pltpu
from jax.sharding import PartitionSpec as P

UNROLL = 32
WINDOW = 48
SUB = 8
LANES = 128


CHUNKS = 8
PACE = 2
SCHED = (("F", 0), ("A", 0), ("B", 1), ("C", 2), ("D", 3), ("E", 4), ("G", 5))
MESH = pl.DeviceIdType.MESH


def lane_index(shape):
    return lax.broadcasted_iota(jnp.int32, shape, len(shape) - 1)


def make_faces(diff, face_x, face_y, size_x, part):
    lane = lane_index((SUB, LANES))
    last = lane == LANES - 1
    at = pl.ds(part * SUB, SUB)

    def step(i, here):
        k0, k1 = here
        n0, n1 = diff[i + 1, 0, at, :], diff[i + 1, 1, at, :]
        face_x[i, 0, at, :] = 0.5 * (k0 + n0)
        face_x[i, 1, at, :] = 0.5 * (k1 + n1)
        r0, r1 = pltpu.roll(k0, LANES - 1, 1), pltpu.roll(k1, LANES - 1, 1)
        face_y[i, 0, at, :] = 0.5 * (k0 + jnp.where(last, r1, r0))
        face_y[i, 1, at, :] = jnp.where(last, 0.0, 0.5 * (k1 + r1))
        return n0, n1

    lax.fori_loop(0, size_x, step, (diff[0, 0, at, :], diff[0, 1, at, :]), unroll=UNROLL)
    face_x[size_x - 1, :, at, :] = jnp.zeros((2, SUB, LANES), jnp.float32)


def clear_edge(ref, first, part):
    shape = (ref.shape[0] - first, *ref.shape[1:-2], SUB, LANES)
    ref[first:, ..., pl.ds(part * SUB, SUB), :] = jnp.zeros(shape, jnp.float32)


def row_of(ref, i, half):
    return (2 * i + half,) if len(ref.shape) == 3 else (i, half)


def diffuse_pass(source, target, face_x, face_y, size_x, part):
    lane = lane_index((SUB, LANES))
    last, first = lane == LANES - 1, lane == 0
    zero = jnp.zeros((SUB, LANES), jnp.float32)
    at = pl.ds(part * SUB, SUB)

    def step(i, carry):
        v0, v1, above0, above1 = carry
        n0, n1 = (source[*row_of(source, i + 1, half), at, :] for half in range(2))
        x0 = face_x[i, 0, at, :] * (n0 - v0)
        x1 = face_x[i, 1, at, :] * (n1 - v1)
        r0, r1 = pltpu.roll(v0, LANES - 1, 1), pltpu.roll(v1, LANES - 1, 1)
        y0 = face_y[i, 0, at, :] * (jnp.where(last, r1, r0) - v0)
        y1 = face_y[i, 1, at, :] * (r1 - v1)
        b0, b1 = pltpu.roll(y0, 1, 1), pltpu.roll(y1, 1, 1)
        target[*row_of(target, i, 0), at, :] = v0 + (x0 - above0) + (y0 - jnp.where(first, b1, b0))
        target[*row_of(target, i, 1), at, :] = v1 + (x1 - above1) + (y1 - jnp.where(first, b0, b1))
        return n0, n1, x0, x1

    begin = (*(source[*row_of(source, 0, half), at, :] for half in range(2)), zero, zero)
    lax.fori_loop(0, size_x, step, begin, unroll=UNROLL)


def by_level(grid, field, sems, part, out=False):
    size_x = grid.shape[1]
    copies = []
    for level in range(part * SUB, (part + 1) * SUB):
        for half in range(2):
            there = grid.at[level, :, pl.ds(half * LANES, LANES)]
            here = field.at[pl.ds(0, size_x), half, level, :]
            pair = (here, there) if out else (there, here)
            copies.append(pltpu.make_async_copy(*pair, sems.at[level, half]))
    return copies


def backward_kernel(
    widths, blocks_in, faces_in, out_to, faces, blocks, one, two, result, sems, out_sems
):
    groups, levels, capacity = blocks.shape
    size_x = out_to.shape[1]
    parts = levels // SUB
    face_x, face_y = faces.at[0], faces.at[1]
    loads = []
    for part in range(parts):
        at = pl.ds(part * SUB, SUB)
        copies = [
            pltpu.make_async_copy(blocks_in.at[:, at, :], blocks.at[:, at, :], sems.at[part, 0]),
            pltpu.make_async_copy(
                faces_in.at[:, :, :, at, :], faces.at[:, :, :, at, :], sems.at[part, 1]
            ),
        ]
        for copy in copies:
            copy.start()
        loads.append(copies)
    lane = lane_index((SUB, LANES))
    outs = []
    for part in range(parts):
        at = pl.ds(part * SUB, SUB)
        loads[part][0].wait()
        end = jnp.int32(0)
        for group in range(groups):
            start, end = end, end + widths[group]
            tile, shift = start // LANES, start % LANES
            keep = lane >= shift

            def place(q, before):
                to = pl.multiple_of(q * LANES, LANES)
                here = pltpu.roll(blocks[group, at, pl.ds(to, LANES)], shift, 1)
                one[tile + q, at, :] = jnp.where(keep, here, before)
                return here

            begin = one[tile, at, :]
            tail = lax.fori_loop(0, capacity // LANES, place, begin, unroll=WINDOW)
            one[tile + capacity // LANES, at, :] = tail
        clear_edge(one, 2 * size_x, part)
        clear_edge(two, 2 * size_x, part)
        loads[part][1].wait()
        for source, target in ((one, two), (two, one), (one, two), (two, result)):
            diffuse_pass(source, target, face_x, face_y, size_x, part)
        copies = by_level(out_to, result, out_sems, part, out=True)
        for copy in copies:
            copy.start()
        outs += copies
    for copy in outs:
        copy.wait()


def split_two(values):
    high = values.astype(jnp.bfloat16)
    low = (values - high.astype(jnp.float32)).astype(jnp.bfloat16)
    return high, low


def main_kernel(
    chunks,
    widths,
    counts,
    control_in,
    diff_in,
    raw,
    perturb_in,
    rinv_in,
    vertical,
    blocks,
    faces_out,
    faces,
    control,
    diff,
    one,
    two,
    pieces,
    slots,
    column,
    perturb,
    rinv,
    weight,
    product,
    from_core,
    half,
    from_z,
    eighth,
    from_x,
    adjoint,
    back,
    field_sem,
    load_sem,
    in_send,
    in_recv,
    out_send,
    out_recv,
    core_send,
    core_recv,
    z_send,
    z_recv,
    x_send,
    x_recv,
):
    groups, levels, capacity = pieces.shape
    size_x = control_in.shape[1]
    tiles = 2 * size_x
    parts = levels // SUB
    total = groups * levels
    rows = capacity // chunks
    face_x, face_y = faces.at[0], faces.at[1]
    diff_copies = [by_level(diff_in, diff, field_sem.at[0], part) for part in range(parts)]
    control_copies = [by_level(control_in, control, field_sem.at[1], part) for part in range(parts)]
    for part in range(parts):
        for copy in diff_copies[part] + control_copies[part]:
            copy.start()
    loads = [
        pltpu.make_async_copy(perturb_in, perturb, load_sem.at[0]),
        pltpu.make_async_copy(rinv_in, rinv, load_sem.at[1]),
    ]
    for copy in loads:
        copy.start()

    mem, lev = lax.axis_index("mem"), lax.axis_index("lev")
    z, x_hi, core = mem // 4, lax.rem(mem // 2, 2), lax.rem(mem, 2)
    other_core = (mem + 1 - 2 * core, lev)
    other_x = (mem + 2 - 4 * x_hi, lev)
    others_z = [lax.rem(z + d, 4) for d in range(1, 4)]
    across_z = [(there * 4 + x_hi * 2 + core, lev) for there in others_z]
    others_lev = [lax.rem(lev + d, groups) for d in range(1, groups)]
    across_lev = [(mem, there) for there in others_lev]
    sources = [lax.rem(lev + groups - d, groups) for d in range(1, groups)]
    barrier = pltpu.get_barrier_semaphore()
    everyone = [other_core, other_x] + across_z + across_lev
    for device in everyone:
        pl.semaphore_signal(barrier, 1, device_id=device, device_id_type=MESH)

    order = lax.broadcasted_iota(jnp.int32, raw.shape, 0) * LANES + lane_index(raw.shape)
    code = lax.rem(raw[...], jnp.full(raw.shape, widths[lev]))
    slots[...] = jnp.where(order < counts[lev], code, -1)
    lane = lane_index((SUB, LANES))

    def smooth(part):
        at = pl.ds(part * SUB, SUB)
        clear_edge(control, size_x, part)
        clear_edge(one, tiles, part)
        clear_edge(two, tiles, part)
        for copy in diff_copies[part]:
            copy.wait()
        make_faces(diff, face_x, face_y, size_x, part)
        for copy in control_copies[part]:
            copy.wait()
        for source, target in ((control, two), (two, one), (one, two), (two, one)):
            diffuse_pass(source, target, face_x, face_y, size_x, part)
        end = jnp.int32(0)
        for group in range(groups):
            start, end = end, end + widths[group]
            tile, shift = start // LANES, start % LANES
            keep = lane < LANES - shift
            back = (LANES - shift) % LANES

            def rolled(t):
                return pltpu.roll(one[t, at, :], back, 1)

            def window(q, here):
                after = rolled(tile + q + 1)
                to = pl.multiple_of(q * LANES, LANES)
                pieces[group, at, pl.ds(to, LANES)] = jnp.where(keep, here, after)
                return after

            lax.fori_loop(0, capacity // LANES, window, rolled(tile), unroll=WINDOW)

    pending = []

    def send(source, target, send_sem, recv_sem, device):
        copy = pltpu.make_async_remote_copy(
            source, target, send_sem, recv_sem, device_id=device, device_id_type=MESH
        )
        copy.start()
        pending.append(copy)

    def arrived(target, recv_sem):
        pltpu.make_async_remote_copy(
            target, target, recv_sem, recv_sem, device_id=other_core, device_id_type=MESH
        ).wait_recv()

    def columns(k):
        return pl.ds(k * rows, rows)

    def enter(k, part):
        at = pl.ds(part * SUB, SUB)
        for d in range(groups - 1):
            send(
                pieces.at[others_lev[d], at, columns(k)],
                column.at[lev, at, columns(k)],
                in_send.at[k, part, d],
                in_recv.at[k, part, d],
                across_lev[d],
            )

    def rows_at(k, *parts):
        first, size = k * rows, rows
        for index, count in parts:
            size = size // count
            first = first + index * size
        return pl.ds(pl.multiple_of(first, 8), size)

    def product_of(high, low, split, contract):
        dims = (((1,), (contract,)), ((), ()))
        v_high, v_low = split
        dot = functools.partial(
            lax.dot_general, dimension_numbers=dims, preferred_element_type=jnp.float32
        )
        return dot(high, v_high) + (dot(high, v_low) + dot(low, v_high))

    for part in range(parts):
        smooth(part)
        if part == 0:
            pl.semaphore_wait(barrier, len(everyone))
        for k in range(min(PACE, chunks)):
            enter(k, part)
    loads.append(pltpu.make_async_copy(pieces.at[lev], column.at[lev], load_sem.at[2]))
    loads.append(pltpu.make_async_copy(faces, faces_out, load_sem.at[3]))
    for copy in loads[2:]:
        copy.start()

    owned = rows // 16
    block = 512
    first_row = core * (rows // 2) + z * (rows // 8) + x_hi * owned
    here = jnp.concatenate(
        [
            first_row + k * rows + lax.broadcasted_iota(jnp.int32, (owned, LANES), 0)
            for k in range(chunks)
        ],
        axis=0,
    )
    loads[1].wait()
    weight[...] = jnp.zeros_like(weight)

    def gather(b, _):
        high, low = split_two(rinv[pl.ds(pl.multiple_of(b * block, block), block), :])
        mine = slots[pl.ds(b * (block // LANES), block // LANES), :]
        chosen = jnp.concatenate(
            [
                jnp.where(here == mine[q : q + 1, :], 1.0, 0.0).astype(jnp.bfloat16)
                for q in range(block // LANES)
            ],
            axis=1,
        )
        dot = functools.partial(jnp.dot, preferred_element_type=jnp.float32)
        weight[...] += dot(chosen, high) + dot(chosen, low)
        return 0

    lax.fori_loop(0, capacity // block, gather, 0)
    split = split_two(vertical[...])
    loads[0].wait()
    loads[2].wait()
    tile = 256

    def contract_in(k):
        for part in range(parts):
            at = pl.ds(part * SUB, SUB)
            for d in range(groups - 1):
                arrived(column.at[sources[d], at, columns(k)], in_recv.at[k, part, d])
        if k + PACE < chunks:
            for part in range(parts):
                enter(k + PACE, part)

        def one(i, _):
            at = pl.ds(pl.multiple_of(k * rows + i * tile, tile), tile)
            high, low = split_two(column[:, :, at].reshape(total, tile).T)
            product[at, :] = perturb[at, :] * product_of(high, low, split, 1)
            return 0

        lax.fori_loop(0, rows // tile, one, 0)
        there = rows_at(k, (1 - core, 2))
        send(product.at[there], from_core.at[k], core_send.at[0, k], core_recv.at[0, k], other_core)

    def add_core(k):
        arrived(from_core.at[k], core_recv.at[0, k])
        half[k] = product[rows_at(k, (core, 2)), :] + from_core[k]
        for d in range(3):
            quarter = half.at[k, pl.ds(pl.multiple_of(others_z[d] * (rows // 8), 8), rows // 8)]
            send(quarter, from_z.at[k, d], z_send.at[0, k, d], z_recv.at[0, k, d], across_z[d])

    def add_z(k):
        for d in range(3):
            arrived(from_z.at[k, d], z_recv.at[0, k, d])
        own = half[k, pl.ds(pl.multiple_of(z * (rows // 8), 8), rows // 8), :]
        eighth[k] = (own + from_z[k, 0]) + (from_z[k, 1] + from_z[k, 2])
        there = eighth.at[k, pl.ds(pl.multiple_of((1 - x_hi) * owned, 8), owned)]
        send(there, from_x.at[k], x_send.at[0, k], x_recv.at[0, k], other_x)

    def add_x(k):
        arrived(from_x.at[k], x_recv.at[0, k])
        own = eighth[k, pl.ds(pl.multiple_of(x_hi * owned, 8), owned), :]
        at = rows_at(k, (core, 2), (z, 4), (x_hi, 2))
        adjoint[at, :] = (own + from_x[k]) * weight[k * owned : (k + 1) * owned, :]
        send(adjoint.at[at], adjoint.at[at], x_send.at[1, k], x_recv.at[1, k], other_x)

    def give_z(k):
        arrived(adjoint.at[rows_at(k, (core, 2), (z, 4), (1 - x_hi, 2))], x_recv.at[1, k])
        at = rows_at(k, (core, 2), (z, 4))
        for d in range(3):
            send(adjoint.at[at], adjoint.at[at], z_send.at[1, k, d], z_recv.at[1, k, d], across_z[d])

    def give_core(k):
        for d in range(3):
            there = lax.rem(z + 3 - d, 4)
            arrived(adjoint.at[rows_at(k, (core, 2), (there, 4))], z_recv.at[1, k, d])
        at = rows_at(k, (core, 2))
        send(adjoint.at[at], adjoint.at[at], core_send.at[1, k], core_recv.at[1, k], other_core)

    def contract_out(k):
        arrived(adjoint.at[rows_at(k, (1 - core, 2))], core_recv.at[1, k])

        def one(i, _):
            at = pl.ds(pl.multiple_of(k * rows + i * tile, tile), tile)
            high, low = split_two(perturb[at, :] * adjoint[at, :])
            back[:, :, at] = product_of(high, low, split, 0).T.reshape(groups, levels, tile)
            return 0

        lax.fori_loop(0, rows // tile, one, 0)
        for d in range(groups - 1):
            send(
                back.at[others_lev[d], :, columns(k)],
                blocks.at[lev, :, columns(k)],
                out_send.at[k, d],
                out_recv.at[k, d],
                across_lev[d],
            )
        pltpu.make_async_copy(
            back.at[lev, :, columns(k)], blocks.at[lev, :, columns(k)], load_sem.at[4 + k]
        ).start()

    stages = dict(F=contract_in, A=add_core, B=add_z, C=add_x, D=give_z, E=give_core, G=contract_out)
    for step in range(chunks + 6):
        for stage, lag in SCHED:
            if 0 <= step - lag < chunks:
                stages[stage](step - lag)

    for k in range(chunks):
        for d in range(groups - 1):
            arrived(blocks.at[sources[d], :, columns(k)], out_recv.at[k, d])
        pltpu.make_async_copy(
            back.at[lev, :, columns(k)], blocks.at[lev, :, columns(k)], load_sem.at[4 + k]
        ).wait()
    loads[3].wait()
    for copy in pending:
        copy.wait_send()


SMEM = pl.BlockSpec(memory_space=pltpu.SMEM)
VMEM = pl.BlockSpec(memory_space=pltpu.VMEM)
ANY = pl.BlockSpec(memory_space=pl.ANY)
LIMIT = 60 * 1024 * 1024


def body(control, diffusivity, perturb, vertical_filter, sub_widths, obs_raw, obs_counts, obs_rinv):
    members, levels, size_x, size_y = control.shape
    capacity = perturb.shape[1]
    groups = sub_widths.shape[0]
    f32 = jnp.float32
    field = pltpu.VMEM((size_x + 1, 2, levels, LANES), f32)
    dma = pltpu.SemaphoreType.DMA
    lines = capacity // LANES
    wide = pltpu.VMEM((2 * size_x + lines + 2, levels, LANES), f32)
    rows = capacity // CHUNKS
    both_faces = (2, size_x, 2, levels, LANES)
    exchange = pltpu.VMEM((groups, levels, capacity), f32)
    blocks, faces = pl.pallas_call(
        functools.partial(main_kernel, CHUNKS),
        out_shape=(
            jax.ShapeDtypeStruct((groups, levels, capacity), f32),
            jax.ShapeDtypeStruct(both_faces, f32),
        ),
        in_specs=[SMEM, SMEM, ANY, ANY, VMEM, ANY, ANY, VMEM],
        out_specs=(ANY, ANY),
        scratch_shapes=[
            pltpu.VMEM(both_faces, f32),
            field,
            field,
            wide,
            wide,
            exchange,
            pltpu.VMEM((lines, LANES), jnp.int32),
            pltpu.VMEM((groups, levels, capacity), f32),
            pltpu.VMEM((capacity, LANES), f32),
            pltpu.VMEM((capacity, LANES), f32),
            pltpu.VMEM((capacity // 16, LANES), f32),
            pltpu.VMEM((capacity, LANES), f32),
            pltpu.VMEM((CHUNKS, rows // 2, LANES), f32),
            pltpu.VMEM((CHUNKS, rows // 2, LANES), f32),
            pltpu.VMEM((CHUNKS, 3, rows // 8, LANES), f32),
            pltpu.VMEM((CHUNKS, rows // 8, LANES), f32),
            pltpu.VMEM((CHUNKS, rows // 16, LANES), f32),
            pltpu.VMEM((capacity, LANES), f32),
            pltpu.VMEM((groups, levels, capacity), f32),
            dma((2, levels, 2)),
            dma((4 + CHUNKS,)),
            dma((CHUNKS, levels // SUB, groups - 1)),
            dma((CHUNKS, levels // SUB, groups - 1)),
            dma((CHUNKS, groups - 1)),
            dma((CHUNKS, groups - 1)),
            dma((2, CHUNKS)),
            dma((2, CHUNKS)),
            dma((2, CHUNKS, 3)),
            dma((2, CHUNKS, 3)),
            dma((2, CHUNKS)),
            dma((2, CHUNKS)),
        ],
        compiler_params=pltpu.CompilerParams(
            vmem_limit_bytes=LIMIT, collective_id=0, has_side_effects=True
        ),
        name="main",
    )(
        sub_widths,
        obs_counts,
        control[0],
        diffusivity,
        obs_raw.reshape(lines, LANES),
        perturb[0],
        obs_rinv[0],
        vertical_filter,
    )

    out = pl.pallas_call(
        backward_kernel,
        out_shape=jax.ShapeDtypeStruct((levels, size_x, size_y), f32),
        in_specs=[SMEM, ANY, ANY],
        out_specs=ANY,
        scratch_shapes=[
            pltpu.VMEM(both_faces, f32),
            exchange,
            wide,
            wide,
            field,
            dma((levels // SUB, 2)),
            dma((levels, 2)),
        ],
        compiler_params=pltpu.CompilerParams(vmem_limit_bytes=LIMIT),
        name="backward",
    )(sub_widths, blocks, faces)
    return out.reshape(control.shape)


def solution(mesh):
    return jax.shard_map(
        body,
        mesh=mesh,
        in_specs=(
            P("mem", "lev", None, None),
            P("lev", None, None),
            P("mem", "lev", None),
            P(),
            P(),
            P("lev", None),
            P(),
            P("lev", None, None),
        ),
        out_specs=P("mem", "lev", None, None),
        check_vma=False,
    )
```

```python
import functools

import jax
import jax.numpy as jnp
from jax import lax
from jax.experimental import pallas as pl
from jax.experimental.pallas import tpu as pltpu
from jax.sharding import PartitionSpec as P

UNROLL = 32
WINDOW = 48
SUB = 8
LANES = 128


CHUNKS = 8
PACE = 3
SCHED = (("F", 0), ("A", 0), ("B", 1), ("C", 3), ("E", 4), ("G", 5))
EARLY = 9
MESH = pl.DeviceIdType.MESH


def lane_index(shape):
    return lax.broadcasted_iota(jnp.int32, shape, len(shape) - 1)


def make_faces(diff, face_x, face_y, size_x, part):
    lane = lane_index((SUB, LANES))
    last = lane == LANES - 1
    at = pl.ds(part * SUB, SUB)

    def step(i, here):
        k0, k1 = here
        n0, n1 = diff[i + 1, 0, at, :], diff[i + 1, 1, at, :]
        face_x[i, 0, at, :] = 0.5 * (k0 + n0)
        face_x[i, 1, at, :] = 0.5 * (k1 + n1)
        r0, r1 = pltpu.roll(k0, LANES - 1, 1), pltpu.roll(k1, LANES - 1, 1)
        face_y[i, 0, at, :] = 0.5 * (k0 + jnp.where(last, r1, r0))
        face_y[i, 1, at, :] = jnp.where(last, 0.0, 0.5 * (k1 + r1))
        return n0, n1

    lax.fori_loop(0, size_x, step, (diff[0, 0, at, :], diff[0, 1, at, :]), unroll=UNROLL)
    face_x[size_x - 1, :, at, :] = jnp.zeros((2, SUB, LANES), jnp.float32)


def clear_edge(ref, first, part):
    shape = (ref.shape[0] - first, *ref.shape[1:-2], SUB, LANES)
    ref[first:, ..., pl.ds(part * SUB, SUB), :] = jnp.zeros(shape, jnp.float32)


def row_of(ref, i, half):
    return (2 * i + half,) if len(ref.shape) == 3 else (i, half)


def diffuse_pass(source, target, face_x, face_y, size_x, part):
    lane = lane_index((SUB, LANES))
    last, first = lane == LANES - 1, lane == 0
    zero = jnp.zeros((SUB, LANES), jnp.float32)
    at = pl.ds(part * SUB, SUB)

    def step(i, carry):
        v0, v1, above0, above1 = carry
        n0, n1 = (source[*row_of(source, i + 1, half), at, :] for half in range(2))
        x0 = face_x[i, 0, at, :] * (n0 - v0)
        x1 = face_x[i, 1, at, :] * (n1 - v1)
        r0, r1 = pltpu.roll(v0, LANES - 1, 1), pltpu.roll(v1, LANES - 1, 1)
        y0 = face_y[i, 0, at, :] * (jnp.where(last, r1, r0) - v0)
        y1 = face_y[i, 1, at, :] * (r1 - v1)
        b0, b1 = pltpu.roll(y0, 1, 1), pltpu.roll(y1, 1, 1)
        target[*row_of(target, i, 0), at, :] = v0 + (x0 - above0) + (y0 - jnp.where(first, b1, b0))
        target[*row_of(target, i, 1), at, :] = v1 + (x1 - above1) + (y1 - jnp.where(first, b0, b1))
        return n0, n1, x0, x1

    begin = (*(source[*row_of(source, 0, half), at, :] for half in range(2)), zero, zero)
    lax.fori_loop(0, size_x, step, begin, unroll=UNROLL)


def by_level(grid, field, sems, part, out=False):
    size_x = grid.shape[1]
    copies = []
    for level in range(part * SUB, (part + 1) * SUB):
        for half in range(2):
            there = grid.at[level, :, pl.ds(half * LANES, LANES)]
            here = field.at[pl.ds(0, size_x), half, level, :]
            pair = (here, there) if out else (there, here)
            copies.append(pltpu.make_async_copy(*pair, sems.at[level, half]))
    return copies


def backward_kernel(
    widths, blocks_in, faces_in, out_to, faces, blocks, one, two, result, sems, out_sems
):
    groups, levels, capacity = blocks.shape
    size_x = out_to.shape[1]
    parts = levels // SUB
    face_x, face_y = faces.at[0], faces.at[1]
    loads = []
    for part in range(parts):
        at = pl.ds(part * SUB, SUB)
        copies = [
            pltpu.make_async_copy(blocks_in.at[:, at, :], blocks.at[:, at, :], sems.at[part, 0]),
            pltpu.make_async_copy(
                faces_in.at[:, :, :, at, :], faces.at[:, :, :, at, :], sems.at[part, 1]
            ),
        ]
        for copy in copies:
            copy.start()
        loads.append(copies)
    lane = lane_index((SUB, LANES))
    outs = []
    for part in range(parts):
        at = pl.ds(part * SUB, SUB)
        loads[part][0].wait()
        end = jnp.int32(0)
        for group in range(groups):
            start, end = end, end + widths[group]
            tile, shift = start // LANES, start % LANES
            keep = lane >= shift

            def place(q, before):
                to = pl.multiple_of(q * LANES, LANES)
                here = pltpu.roll(blocks[group, at, pl.ds(to, LANES)], shift, 1)
                one[tile + q, at, :] = jnp.where(keep, here, before)
                return here

            begin = one[tile, at, :]
            tail = lax.fori_loop(0, capacity // LANES, place, begin, unroll=WINDOW)
            one[tile + capacity // LANES, at, :] = tail
        clear_edge(one, 2 * size_x, part)
        clear_edge(two, 2 * size_x, part)
        loads[part][1].wait()
        for source, target in ((one, two), (two, one), (one, two), (two, result)):
            diffuse_pass(source, target, face_x, face_y, size_x, part)
        copies = by_level(out_to, result, out_sems, part, out=True)
        for copy in copies:
            copy.start()
        outs += copies
    for copy in outs:
        copy.wait()


def split_two(values):
    high = values.astype(jnp.bfloat16)
    low = (values - high.astype(jnp.float32)).astype(jnp.bfloat16)
    return high, low


def main_kernel(
    chunks,
    widths,
    counts,
    control_in,
    diff_in,
    raw,
    perturb_in,
    rinv_in,
    vertical,
    blocks,
    faces_out,
    faces,
    control,
    diff,
    one,
    two,
    pieces,
    slots,
    column,
    perturb,
    rinv,
    weight,
    product,
    from_core,
    half,
    from_z,
    eighth,
    from_x,
    adjoint,
    back,
    field_sem,
    load_sem,
    in_send,
    in_recv,
    out_send,
    out_recv,
    core_send,
    core_recv,
    z_send,
    z_recv,
    x_send,
    x_recv,
):
    groups, levels, capacity = pieces.shape
    size_x = control_in.shape[1]
    tiles = 2 * size_x
    parts = levels // SUB
    total = groups * levels
    rows = capacity // chunks
    face_x, face_y = faces.at[0], faces.at[1]
    diff_copies = [by_level(diff_in, diff, field_sem.at[0], part) for part in range(parts)]
    control_copies = [by_level(control_in, control, field_sem.at[1], part) for part in range(parts)]
    for part in range(parts):
        for copy in diff_copies[part] + control_copies[part]:
            copy.start()
    loads = [
        pltpu.make_async_copy(perturb_in, perturb, load_sem.at[0]),
        pltpu.make_async_copy(rinv_in, rinv, load_sem.at[1]),
    ]
    for copy in loads:
        copy.start()

    mem, lev = lax.axis_index("mem"), lax.axis_index("lev")
    z, x_hi, core = mem // 4, lax.rem(mem // 2, 2), lax.rem(mem, 2)
    other_core = (mem + 1 - 2 * core, lev)
    other_x = (mem + 2 - 4 * x_hi, lev)
    others_z = [lax.rem(z + d, 4) for d in range(1, 4)]
    across_z = [(there * 4 + x_hi * 2 + core, lev) for there in others_z]
    others_lev = [lax.rem(lev + d, groups) for d in range(1, groups)]
    across_lev = [(mem, there) for there in others_lev]
    sources = [lax.rem(lev + groups - d, groups) for d in range(1, groups)]
    barrier = pltpu.get_barrier_semaphore()
    everyone = [other_core, other_x] + across_z + across_lev
    for device in everyone:
        pl.semaphore_signal(barrier, 1, device_id=device, device_id_type=MESH)

    order = lax.broadcasted_iota(jnp.int32, raw.shape, 0) * LANES + lane_index(raw.shape)
    code = lax.rem(raw[...], jnp.full(raw.shape, widths[lev]))
    slots[...] = jnp.where(order < counts[lev], code, -1)
    lane = lane_index((SUB, LANES))

    def smooth(part):
        at = pl.ds(part * SUB, SUB)
        clear_edge(control, size_x, part)
        clear_edge(one, tiles, part)
        clear_edge(two, tiles, part)
        for copy in diff_copies[part]:
            copy.wait()
        make_faces(diff, face_x, face_y, size_x, part)
        for copy in control_copies[part]:
            copy.wait()
        for source, target in ((control, two), (two, one), (one, two), (two, one)):
            diffuse_pass(source, target, face_x, face_y, size_x, part)
        end = jnp.int32(0)
        for group in range(groups):
            start, end = end, end + widths[group]
            tile, shift = start // LANES, start % LANES
            keep = lane < LANES - shift
            back = (LANES - shift) % LANES

            def rolled(t):
                return pltpu.roll(one[t, at, :], back, 1)

            def window(q, here):
                after = rolled(tile + q + 1)
                to = pl.multiple_of(q * LANES, LANES)
                pieces[group, at, pl.ds(to, LANES)] = jnp.where(keep, here, after)
                return after

            lax.fori_loop(0, capacity // LANES, window, rolled(tile), unroll=WINDOW)

    pending = []

    def send(source, target, send_sem, recv_sem, device):
        copy = pltpu.make_async_remote_copy(
            source, target, send_sem, recv_sem, device_id=device, device_id_type=MESH
        )
        copy.start()
        pending.append(copy)

    def arrived(target, recv_sem):
        pltpu.make_async_remote_copy(
            target, target, recv_sem, recv_sem, device_id=other_core, device_id_type=MESH
        ).wait_recv()

    def columns(k):
        return pl.ds(k * rows, rows)

    def enter(k, part):
        at = pl.ds(part * SUB, SUB)
        for d in range(groups - 1):
            send(
                pieces.at[others_lev[d], at, columns(k)],
                column.at[lev, at, columns(k)],
                in_send.at[k, part, d],
                in_recv.at[k, part, d],
                across_lev[d],
            )

    def rows_at(k, *parts):
        first, size = k * rows, rows
        for index, count in parts:
            size = size // count
            first = first + index * size
        return pl.ds(pl.multiple_of(first, 8), size)

    def product_of(high, low, split, contract):
        dims = (((1,), (contract,)), ((), ()))
        v_high, v_low = split
        dot = functools.partial(
            lax.dot_general, dimension_numbers=dims, preferred_element_type=jnp.float32
        )
        return dot(high, v_high) + (dot(high, v_low) + dot(low, v_high))

    for part in range(parts):
        smooth(part)
        if part == 0:
            pl.semaphore_wait(barrier, len(everyone))
        for k in range(min(PACE, chunks)):
            enter(k, part)
    loads.append(pltpu.make_async_copy(pieces.at[lev], column.at[lev], load_sem.at[2]))
    loads.append(pltpu.make_async_copy(faces, faces_out, load_sem.at[3]))
    for copy in loads[2:]:
        copy.start()

    owned = rows // 8
    block = 512
    first_row = core * (rows // 2) + z * owned
    here = jnp.concatenate(
        [
            first_row + k * rows + lax.broadcasted_iota(jnp.int32, (owned, LANES), 0)
            for k in range(chunks)
        ],
        axis=0,
    )
    loads[1].wait()
    weight[...] = jnp.zeros_like(weight)

    def gather(b, _):
        high, low = split_two(rinv[pl.ds(pl.multiple_of(b * block, block), block), :])
        mine = slots[pl.ds(b * (block // LANES), block // LANES), :]
        chosen = jnp.concatenate(
            [
                jnp.where(here == mine[q : q + 1, :], 1.0, 0.0).astype(jnp.bfloat16)
                for q in range(block // LANES)
            ],
            axis=1,
        )
        both = jnp.concatenate([high, low], axis=1)
        found = jnp.dot(chosen, both, preferred_element_type=jnp.float32)
        weight[...] += found[:, :LANES] + found[:, LANES:]
        return 0

    gathers = capacity // block
    lax.fori_loop(0, EARLY, gather, 0)
    split = split_two(vertical[...])
    loads[0].wait()
    loads[2].wait()
    tile = 256

    def contract_in(k):
        for part in range(parts):
            at = pl.ds(part * SUB, SUB)
            for d in range(groups - 1):
                arrived(column.at[sources[d], at, columns(k)], in_recv.at[k, part, d])
        if k + PACE < chunks:
            for part in range(parts):
                enter(k + PACE, part)

        def one(i, _):
            at = pl.ds(pl.multiple_of(k * rows + i * tile, tile), tile)
            high, low = split_two(column[:, :, at].reshape(total, tile).T)
            product[at, :] = perturb[at, :] * product_of(high, low, split, 1)
            return 0

        lax.fori_loop(0, rows // tile, one, 0)
        there = rows_at(k, (1 - core, 2))
        send(product.at[there], from_core.at[k], core_send.at[0, k], core_recv.at[0, k], other_core)

    def add_core(k):
        arrived(from_core.at[k], core_recv.at[0, k])
        half[k] = product[rows_at(k, (core, 2)), :] + from_core[k]
        for d in range(3):
            quarter = half.at[k, pl.ds(pl.multiple_of(others_z[d] * (rows // 8), 8), rows // 8)]
            send(quarter, from_z.at[k, d], z_send.at[0, k, d], z_recv.at[0, k, d], across_z[d])

    def add_z(k):
        for d in range(3):
            arrived(from_z.at[k, d], z_recv.at[0, k, d])
        own = half[k, pl.ds(pl.multiple_of(z * (rows // 8), 8), rows // 8), :]
        eighth[k] = (own + from_z[k, 0]) + (from_z[k, 1] + from_z[k, 2])
        send(eighth.at[k], from_x.at[k], x_send.at[k], x_recv.at[k], other_x)

    def add_x(k):
        arrived(from_x.at[k], x_recv.at[k])
        at = rows_at(k, (core, 2), (z, 4))
        adjoint[at, :] = (eighth[k] + from_x[k]) * weight[k * owned : (k + 1) * owned, :]
        for d in range(3):
            send(adjoint.at[at], adjoint.at[at], z_send.at[1, k, d], z_recv.at[1, k, d], across_z[d])

    def give_core(k):
        for d in range(3):
            there = lax.rem(z + 3 - d, 4)
            arrived(adjoint.at[rows_at(k, (core, 2), (there, 4))], z_recv.at[1, k, d])
        at = rows_at(k, (core, 2))
        send(adjoint.at[at], adjoint.at[at], core_send.at[1, k], core_recv.at[1, k], other_core)

    def contract_out(k):
        arrived(adjoint.at[rows_at(k, (1 - core, 2))], core_recv.at[1, k])

        def one(i, _):
            at = pl.ds(pl.multiple_of(k * rows + i * tile, tile), tile)
            high, low = split_two(perturb[at, :] * adjoint[at, :])
            back[:, :, at] = product_of(high, low, split, 0).T.reshape(groups, levels, tile)
            return 0

        lax.fori_loop(0, rows // tile, one, 0)
        for d in range(groups - 1):
            send(
                back.at[others_lev[d], :, columns(k)],
                blocks.at[lev, :, columns(k)],
                out_send.at[k, d],
                out_recv.at[k, d],
                across_lev[d],
            )
        pltpu.make_async_copy(
            back.at[lev, :, columns(k)], blocks.at[lev, :, columns(k)], load_sem.at[4 + k]
        ).start()

    stages = dict(F=contract_in, A=add_core, B=add_z, C=add_x, E=give_core, G=contract_out)
    for step in range(chunks + 6):
        for stage, lag in SCHED:
            if 0 <= step - lag < chunks:
                stages[stage](step - lag)
        if step == 0:
            lax.fori_loop(EARLY, gathers, gather, 0)

    for k in range(chunks):
        for d in range(groups - 1):
            arrived(blocks.at[sources[d], :, columns(k)], out_recv.at[k, d])
        pltpu.make_async_copy(
            back.at[lev, :, columns(k)], blocks.at[lev, :, columns(k)], load_sem.at[4 + k]
        ).wait()
    loads[3].wait()
    for copy in pending:
        copy.wait_send()


SMEM = pl.BlockSpec(memory_space=pltpu.SMEM)
VMEM = pl.BlockSpec(memory_space=pltpu.VMEM)
ANY = pl.BlockSpec(memory_space=pl.ANY)
LIMIT = 60 * 1024 * 1024


def body(control, diffusivity, perturb, vertical_filter, sub_widths, obs_raw, obs_counts, obs_rinv):
    members, levels, size_x, size_y = control.shape
    capacity = perturb.shape[1]
    groups = sub_widths.shape[0]
    f32 = jnp.float32
    field = pltpu.VMEM((size_x + 1, 2, levels, LANES), f32)
    dma = pltpu.SemaphoreType.DMA
    lines = capacity // LANES
    wide = pltpu.VMEM((2 * size_x + lines + 2, levels, LANES), f32)
    rows = capacity // CHUNKS
    both_faces = (2, size_x, 2, levels, LANES)
    exchange = pltpu.VMEM((groups, levels, capacity), f32)
    blocks, faces = pl.pallas_call(
        functools.partial(main_kernel, CHUNKS),
        out_shape=(
            jax.ShapeDtypeStruct((groups, levels, capacity), f32),
            jax.ShapeDtypeStruct(both_faces, f32),
        ),
        in_specs=[SMEM, SMEM, ANY, ANY, VMEM, ANY, ANY, VMEM],
        out_specs=(ANY, ANY),
        scratch_shapes=[
            pltpu.VMEM(both_faces, f32),
            field,
            field,
            wide,
            wide,
            exchange,
            pltpu.VMEM((lines, LANES), jnp.int32),
            pltpu.VMEM((groups, levels, capacity), f32),
            pltpu.VMEM((capacity, LANES), f32),
            pltpu.VMEM((capacity, LANES), f32),
            pltpu.VMEM((capacity // 8, LANES), f32),
            pltpu.VMEM((capacity, LANES), f32),
            pltpu.VMEM((CHUNKS, rows // 2, LANES), f32),
            pltpu.VMEM((CHUNKS, rows // 2, LANES), f32),
            pltpu.VMEM((CHUNKS, 3, rows // 8, LANES), f32),
            pltpu.VMEM((CHUNKS, rows // 8, LANES), f32),
            pltpu.VMEM((CHUNKS, rows // 8, LANES), f32),
            pltpu.VMEM((capacity, LANES), f32),
            pltpu.VMEM((groups, levels, capacity), f32),
            dma((2, levels, 2)),
            dma((4 + CHUNKS,)),
            dma((CHUNKS, levels // SUB, groups - 1)),
            dma((CHUNKS, levels // SUB, groups - 1)),
            dma((CHUNKS, groups - 1)),
            dma((CHUNKS, groups - 1)),
            dma((2, CHUNKS)),
            dma((2, CHUNKS)),
            dma((2, CHUNKS, 3)),
            dma((2, CHUNKS, 3)),
            dma((CHUNKS,)),
            dma((CHUNKS,)),
        ],
        compiler_params=pltpu.CompilerParams(
            vmem_limit_bytes=LIMIT, collective_id=0, has_side_effects=True
        ),
        name="main",
    )(
        sub_widths,
        obs_counts,
        control[0],
        diffusivity,
        obs_raw.reshape(lines, LANES),
        perturb[0],
        obs_rinv[0],
        vertical_filter,
    )

    out = pl.pallas_call(
        backward_kernel,
        out_shape=jax.ShapeDtypeStruct((levels, size_x, size_y), f32),
        in_specs=[SMEM, ANY, ANY],
        out_specs=ANY,
        scratch_shapes=[
            pltpu.VMEM(both_faces, f32),
            exchange,
            wide,
            wide,
            field,
            dma((levels // SUB, 2)),
            dma((levels, 2)),
        ],
        compiler_params=pltpu.CompilerParams(vmem_limit_bytes=LIMIT),
        name="backward",
    )(sub_widths, blocks, faces)
    return out.reshape(control.shape)


def solution(mesh):
    return jax.shard_map(
        body,
        mesh=mesh,
        in_specs=(
            P("mem", "lev", None, None),
            P("lev", None, None),
            P("mem", "lev", None),
            P(),
            P(),
            P("lev", None),
            P(),
            P("lev", None, None),
        ),
        out_specs=P("mem", "lev", None, None),
        check_vma=False,
    )
```
